256 devices in a mesh: tm: 32 (over z, y), space: 8 (over x, core).
Axes of the slice: x: 4, y: 4, z: 8, core: 2. Of those that a mesh axis runs over, the one named last changes fastest.
Arguments:
- video: bfloat16 [128, 64, 64, 256], P('tm', 'space'), may hold values from -6 to 6
- cotangent: bfloat16 [128, 64, 64, 256], P('tm', 'space'), may hold values from -6 to 6
- frame_count: int32 [32], replicated, may hold values from 1 to 4, 96 in all
- row_count: int32 [8], replicated, may hold values from 1 to 8, 48 in all
- w_conv: bfloat16 [3, 3, 256, 256], replicated, may hold values from -0.125 to 0.125
- w_query: bfloat16 [256, 256], replicated, may hold values from -1 to 1
- w_key: bfloat16 [256, 256], replicated, may hold values from -1 to 1
- w_value: bfloat16 [256, 256], replicated, may hold values from -0.375 to 0.375
- w_out: bfloat16 [256, 256], replicated, may hold values from -0.375 to 0.375
Outputs:
- encoded: bfloat16 [128, 64, 64, 256], P('tm', 'space')
- video_grad: bfloat16 [128, 64, 64, 256], P('tm', 'space')
The draws below stay inside these ranges and needn't reach their ends.
Inputs may be any that keep to these rules, and one draw needn't show every extreme that they name: `frame_count`: the counts sum to 3 times the number of time blocks, and the largest is 4. `row_count`: the counts sum to 6 times the number of spatial tiles, and the largest is 8.
All inputs are finite; a program needn't handle non-finite values.
Results may differ from the reference program's by a relative error of at most 0.011.
Values may be sent and summed in bfloat16 or wider, within the bound.
No kernel may reach another device: no remote copies, remote signals or barrier semaphores. Data moves between devices by JAX's collectives and lax.ppermute only.
A program may use at most 64 MiB of HBM per device.

```python
import math
import jax
import jax.numpy as jnp
import numpy as np
from jax import lax

C = 256
FCAP = 4
RCAP = 8
W = 64
FRAMES = 128
ROWS = 64
N_TM = 32
N_SPACE = 8


def shared_parts(key):
    base = jnp.clip(jax.random.normal(jax.random.fold_in(key, 11), (C, C), jnp.float32), -4.0, 4.0)
    noise = jnp.clip(jax.random.normal(jax.random.fold_in(key, 12), (C, C), jnp.float32), -4.0, 4.0)
    return (base, noise)


def draw_w_query(key, part):
    base, noise = shared_parts(key)
    values = base
    return jnp.clip(values / math.sqrt(C), -1.0, 1.0).astype(jnp.bfloat16)


def draw_w_key(key, part):
    base, noise = shared_parts(key)
    values = noise
    return jnp.clip(values / math.sqrt(C), -1.0, 1.0).astype(jnp.bfloat16)


def block_scale(key, extent, split, smallest, top_value):
    loudness, own = 1.0, jax.random.fold_in(key, 6)
    for position, shards_of in split:
        steps = jnp.exp(jax.random.uniform(jax.random.fold_in(own, position), (shards_of,), jnp.float32, smallest / len(split), top_value / len(split)))
        loudness = loudness * jnp.repeat(steps, extent[position] // shards_of).reshape([-1 if axis == position else 1 for axis in range(len(extent))])
    return loudness


def profile(amount, total, limit, slope):
    portions = [(1 << 20) // math.isqrt(grade ** slope) + 1 for grade in range(2, amount + 1)]
    surplus, holding = total - limit - (amount - 1), [1] * (amount - 1)
    while surplus > 0:
        free = [i for i in range(amount - 1) if holding[i] < limit]
        mass, budget = sum([portions[i] for i in free]), surplus
        for i in free:
            more = min(limit - holding[i], max(1, budget * portions[i] // mass), surplus)
            holding[i] = holding[i] + more
            surplus = surplus - more
    return np.array([limit] + holding)


def uneven(own_key, count, total, bound, skew):
    if count == 2:
        one = jax.random.randint(own_key, (), max(1, total - bound), min(bound, total - 1) + 1)
        return jnp.stack([one, total - one])
    lengths = jnp.asarray(profile(count, total, bound, skew), jnp.int32)
    pairs = (count - 1) // 2
    giver, taker = lengths[1:1 + 2 * pairs:2], lengths[2:2 + 2 * pairs:2]
    room = jnp.minimum(giver - 1, bound - taker)
    passed = jax.random.randint(jax.random.fold_in(own_key, 1), (pairs,), 0, 1 << 20) % (room + 1)
    lengths = lengths.at[1:1 + 2 * pairs:2].set(giver - passed).at[2:2 + 2 * pairs:2].set(taker + passed)
    return lengths[jax.random.permutation(jax.random.fold_in(own_key, 2), count)]


def normal_values(key, extent, scale, most, pieces=(), held_as=jnp.bfloat16):
    values = jax.random.normal(key, extent, jnp.float32) * scale
    if len(pieces) > 0:
        values = block_scale(key, extent, pieces, -0.22, 0.18) * values
    return jnp.clip(values, min=-most, max=most).astype(held_as)


def setup_inputs(seed: int = 0) -> dict:
    key_of = jax.random.split(jax.random.key(seed), 10)
    return {
        "video": normal_values(key_of[0], (FRAMES, ROWS, W, C), 1.0, 6.0, ((0, 32), (1, 8))),
        "cotangent": normal_values(key_of[1], (FRAMES, ROWS, W, C), 1.0, 6.0, ((0, 32), (1, 8))),
        "frame_count": uneven(key_of[2], N_TM, 3 * N_TM, FCAP, 1).astype(jnp.int32),
        "row_count": uneven(key_of[3], N_SPACE, 6 * N_SPACE, RCAP, 1).astype(jnp.int32),
        "w_conv": normal_values(key_of[4], (3, 3, C, C), (9 * C) ** -0.5, 0.125),
        "w_query": draw_w_query(jax.random.fold_in(key_of[9], 71), 0),
        "w_key": draw_w_key(jax.random.fold_in(key_of[9], 71), 0),
        "w_value": normal_values(key_of[7], (C, C), C ** -0.5, 0.375),
        "w_out": normal_values(key_of[8], (C, C), C ** -0.5, 0.375),
    }


def neighbour_rows(row_count):
    index = jnp.arange(ROWS, dtype=jnp.int32)
    tile = index // RCAP
    local = index % RCAP
    count = row_count[tile]
    used = local < count
    prev_count = row_count[jnp.maximum(tile - 1, 0)]
    prev_index = jnp.where(local > 0, index - 1, (tile - 1) * RCAP + prev_count - 1)
    has_prev = (local > 0) | (tile > 0)
    next_index = jnp.where(local < count - 1, index + 1, (tile + 1) * RCAP)
    has_next = (local < count - 1) | (tile < N_SPACE - 1)
    prev_index = jnp.clip(prev_index, 0, ROWS - 1).astype(jnp.int32)
    next_index = jnp.clip(next_index, 0, ROWS - 1).astype(jnp.int32)
    return (used, prev_index, has_prev, next_index, has_next)

def shift_cols(field):
    zero_col = jnp.zeros_like(field[:, :, :1])
    left = jnp.concatenate([zero_col, field[:, :, :-1]], axis=2)
    right = jnp.concatenate([field[:, :, 1:], zero_col], axis=2)
    return jnp.stack([left, field, right], axis=3)

def convolve(field, weight, links):
    used, prev_index, has_prev, next_index, has_next = links
    upper = jnp.where(has_prev[None, :, None, None], jnp.take(field, prev_index, axis=1), jnp.zeros_like(field))
    lower = jnp.where(has_next[None, :, None, None], jnp.take(field, next_index, axis=1), jnp.zeros_like(field))
    total = jnp.zeros(field.shape, jnp.float32)
    for offset, view in enumerate((upper, field, lower)):
        total = total + jnp.einsum('frwbc,bcd->frwd', shift_cols(view).astype(jnp.float32), weight[offset].astype(jnp.float32))
    return total

def reference(video, cotangent, frame_count, row_count, w_conv, w_query, w_key, w_value, w_out):
    links = neighbour_rows(row_count)
    frame_index = jnp.arange(FRAMES, dtype=jnp.int32)
    frame_used = frame_index % FCAP < frame_count[frame_index // FCAP]
    mask = (frame_used[:, None] & links[0][None, :]).astype(jnp.float32)[:, :, None, None]
    masked = (video.astype(jnp.float32) * mask).astype(jnp.bfloat16)
    hidden = ((masked.astype(jnp.float32) + convolve(masked, w_conv, links)) * mask).astype(jnp.bfloat16)
    hidden_f = hidden.astype(jnp.float32)
    inv_rms = lax.rsqrt(lax.optimization_barrier(jnp.mean(hidden_f * hidden_f, axis=-1, keepdims=True)) + 1e-06)
    normed = (hidden_f * inv_rms).astype(jnp.bfloat16)
    positions = ROWS * W
    flat = normed.reshape(FRAMES, positions, C)
    queries = jnp.dot(flat, w_query, preferred_element_type=jnp.float32).astype(jnp.bfloat16)
    key_rows = jnp.dot(flat, w_key, preferred_element_type=jnp.float32).astype(jnp.bfloat16)
    value_rows = jnp.dot(flat, w_value, preferred_element_type=jnp.float32).astype(jnp.bfloat16)
    scale = C ** (-0.5)
    scores = jnp.einsum('fpc,gpc->pfg', queries.astype(jnp.float32), key_rows.astype(jnp.float32)) * scale
    allowed = (frame_index[None, :] <= frame_index[:, None]) & frame_used[None, :]
    scores = jnp.where(allowed[None], scores, -1e+30)
    top = lax.optimization_barrier(jnp.max(scores, axis=-1, keepdims=True))
    expo = jnp.exp(scores - top)
    probs = expo / lax.optimization_barrier(jnp.sum(expo, axis=-1, keepdims=True))
    probs_low = probs.astype(jnp.bfloat16)
    attended = jnp.einsum('pfg,gpc->fpc', probs_low.astype(jnp.float32), value_rows.astype(jnp.float32)).astype(jnp.bfloat16)
    projected = jnp.dot(attended, w_out, preferred_element_type=jnp.float32).astype(jnp.bfloat16)
    projected = projected.reshape(FRAMES, ROWS, W, C)
    encoded = ((hidden_f + projected.astype(jnp.float32)) * mask).astype(jnp.bfloat16)
    grad_out = (cotangent.astype(jnp.float32) * mask).astype(jnp.bfloat16)
    grad_attended = jnp.dot(grad_out.reshape(FRAMES, positions, C), w_out.T, preferred_element_type=jnp.float32).astype(jnp.bfloat16)
    grad_probs = jnp.einsum('fpc,gpc->pfg', grad_attended.astype(jnp.float32), value_rows.astype(jnp.float32))
    delta = lax.optimization_barrier(jnp.sum(grad_attended.astype(jnp.float32) * attended.astype(jnp.float32), axis=-1)).T[:, :, None]
    grad_scores = (probs * (grad_probs - delta) * scale).astype(jnp.bfloat16)
    grad_queries = jnp.einsum('pfg,gpc->fpc', grad_scores.astype(jnp.float32), key_rows.astype(jnp.float32)).astype(jnp.bfloat16)
    grad_keys = jnp.einsum('pfg,fpc->gpc', grad_scores.astype(jnp.float32), queries.astype(jnp.float32)).astype(jnp.bfloat16)
    grad_values = jnp.einsum('pfg,fpc->gpc', probs_low.astype(jnp.float32), grad_attended.astype(jnp.float32)).astype(jnp.bfloat16)
    grad_normed = jnp.dot(grad_queries, w_query.T, preferred_element_type=jnp.float32)
    grad_normed = grad_normed + jnp.dot(grad_keys, w_key.T, preferred_element_type=jnp.float32)
    grad_normed = grad_normed + jnp.dot(grad_values, w_value.T, preferred_element_type=jnp.float32)
    grad_normed = grad_normed.astype(jnp.bfloat16).reshape(FRAMES, ROWS, W, C).astype(jnp.float32)
    inner = lax.optimization_barrier(jnp.mean(grad_normed * hidden_f, axis=-1, keepdims=True))
    grad_hidden = (mask * (grad_out.astype(jnp.float32) + inv_rms * grad_normed - inv_rms ** 3 * hidden_f * inner)).astype(jnp.bfloat16)
    flipped = jnp.transpose(jnp.flip(w_conv, (0, 1)), (0, 1, 3, 2))
    video_grad = (mask * (grad_hidden.astype(jnp.float32) + convolve(grad_hidden, flipped, links))).astype(jnp.bfloat16)
    return (encoded, video_grad)
```

```python
import functools

import jax
import jax.numpy as jnp
from jax import lax
from jax.experimental import pallas as pl
from jax.experimental.pallas import tpu as pltpu
from jax.sharding import PartitionSpec as P

BF16 = jnp.bfloat16
F32 = jnp.float32
GROUP = 4
LANES = 128
VMEM = pltpu.VMEM
SMEM = pltpu.SMEM


def dot(a, b, contract=(1, 0)):
    return lax.dot_general(
        a, b, (((contract[0],), (contract[1],)), ((), ())), preferred_element_type=F32
    )


def specs(*spaces):
    return [pl.BlockSpec(memory_space=space) for space in spaces]


def cost(flops, moved):
    return pl.CostEstimate(flops=flops, bytes_accessed=moved, transcendentals=0)


def edges_kernel(row_count, field, head, tail, sems):
    rows_here = row_count[lax.axis_index("space")]
    first = pltpu.make_async_copy(field.at[:, 0], head, sems.at[0])
    last = pltpu.make_async_copy(field.at[:, rows_here - 1], tail, sems.at[1])
    first.start()
    last.start()
    first.wait()
    last.wait()


def fill_halo(extended, field, above, below, rows_here):
    slots = field.shape[1]
    extended[:, 1 : 1 + slots] = field[...]
    extended[:, 0] = above[...]
    extended[:, 1 + rows_here] = below[...]


def convolve_frame(extended, weight, frame, flipped):
    _, padded, columns, channels = extended.shape
    tokens = (padded - 2) * columns
    column = lax.broadcasted_iota(jnp.int32, (tokens, channels), 0) % columns
    total = None
    for b in range(3):
        part = None
        for a in range(3):
            view = extended[frame, a : a + padded - 2].reshape(tokens, channels)
            if flipped:
                term = dot(view, weight[2 - a, 2 - b], (1, 1))
            else:
                term = dot(view, weight[a, b])
            part = term if part is None else part + term
        if b == 0:
            part = jnp.where(column == 0, 0.0, pltpu.roll(part, 1, 0))
        elif b == 2:
            part = jnp.where(column == columns - 1, 0.0, pltpu.roll(part, tokens - 1, 0))
        total = part if total is None else total + part
    return total


def token_mask(frame, frames_here, rows_here, columns, shape):
    row = lax.broadcasted_iota(jnp.int32, shape, 0) // columns
    return (row < rows_here) & (frame < frames_here)


def inverse_rms(hidden):
    return lax.rsqrt(jnp.mean(hidden * hidden, axis=-1, keepdims=True) + 1e-06)


def hidden_kernel(
    frame_count, row_count, field, above, below, weight, hidden_out, normed_out, extended
):
    frames_here = frame_count[lax.axis_index("tm")]
    rows_here = row_count[lax.axis_index("space")]
    frames, slots, columns, channels = field.shape
    tokens = slots * columns
    fill_halo(extended, field, above, below, rows_here)

    def step(frame, carry):
        total = convolve_frame(extended, weight, frame, False)
        used = token_mask(frame, frames_here, rows_here, columns, total.shape)
        center = field[frame].reshape(tokens, channels).astype(F32)
        hidden = jnp.where(used, center + total, 0.0).astype(BF16)
        hidden_out[:, frame] = hidden.reshape(hidden_out.shape[0], -1, channels)
        hidden_f = hidden.astype(F32)
        normed = (hidden_f * inverse_rms(hidden_f)).astype(BF16)
        normed_out[:, frame] = normed.reshape(normed_out.shape[0], -1, channels)
        return carry

    lax.fori_loop(0, frames, step, 0)


def by_position(source, spread, target, scale=None):
    frames, positions, channels = source.shape
    for h in range(channels // LANES):
        lanes = slice(h * LANES, (h + 1) * LANES)
        part = source[:, :, lanes].astype(F32)
        spread[h] = part.reshape(frames * positions, LANES)
        for p in range(positions):
            rows = spread[h, pl.ds(p, frames, stride=positions), :]
            if scale is not None:
                rows = rows * scale
            target[p, :, lanes] = rows.astype(BF16)


def scatter_position(spread, position, positions, rows):
    for h in range(spread.shape[0]):
        part = rows[:, h * LANES : (h + 1) * LANES]
        spread[h, pl.ds(position, rows.shape[0], stride=positions), :] = part


def gather_frames(spread, target):
    for h in range(spread.shape[0]):
        part = spread[h].reshape(target.shape[0], target.shape[1], LANES)
        target[:, :, h * LANES : (h + 1) * LANES] = part.astype(BF16)


def grads_kernel(cotangent, used, w_out, grad_out, spread, ordered):
    by_position(cotangent, spread, ordered, used[...])
    positions, frames, channels = ordered.shape

    def step(i, carry):
        rows = ordered[pl.ds(i * GROUP, GROUP)].reshape(GROUP * frames, channels)
        grads = dot(rows, w_out[...], (1, 1)).astype(BF16)
        grad_out[pl.ds(i * GROUP, GROUP)] = grads.reshape(GROUP, frames, channels)
        return carry

    lax.fori_loop(0, positions // GROUP, step, 0)


def attention_kernel(
    normed, grads, used, w_query, w_key, w_value, attended, grad_normed,
    spread, ordered, query_s, key_s, value_s, dq_s, dk_s, dv_s,
):
    all_frames, positions, channels = normed.shape
    by_position(normed, spread, ordered)
    tile = (all_frames, all_frames)
    source = lax.broadcasted_iota(jnp.int32, tile, 0)
    reader = lax.broadcasted_iota(jnp.int32, tile, 1)
    allowed = (source <= reader) & (used[...] > 0.0)
    scale = channels ** (-0.5)

    def step(i, carry):
        rows = ordered[pl.ds(i * GROUP, GROUP)].reshape(GROUP * all_frames, channels)
        query_s[...] = dot(rows, w_query[...]).astype(BF16)
        key_s[...] = dot(rows, w_key[...]).astype(BF16)
        value_s[...] = dot(rows, w_value[...]).astype(BF16)
        for j in range(GROUP):
            here = pl.ds(j * all_frames, all_frames)
            query, key, value = query_s[here], key_s[here], value_s[here]
            grad = grads[i * GROUP + j]
            scores = jnp.where(allowed, dot(key, query, (1, 1)) * scale, -1e30)
            expo = jnp.exp(scores - jnp.max(scores, axis=0, keepdims=True))
            probs = expo * (1.0 / jnp.sum(expo, axis=0, keepdims=True))
            low = probs.astype(BF16)
            attended[i * GROUP + j] = dot(low, value, (0, 0)).astype(BF16)
            grad_probs = dot(value, grad, (1, 1))
            delta = jnp.sum(low.astype(F32) * grad_probs, axis=0, keepdims=True)
            grad_scores = (probs * (grad_probs - delta) * scale).astype(BF16)
            dv_s[here] = dot(low, grad).astype(BF16)
            dk_s[here] = dot(grad_scores, query).astype(BF16)
            dq_s[here] = dot(grad_scores, key, (0, 0)).astype(BF16)
        total = dot(dq_s[...], w_query[...], (1, 1))
        total = total + dot(dk_s[...], w_key[...], (1, 1))
        total = total + dot(dv_s[...], w_value[...], (1, 1))
        total = total.astype(BF16).astype(F32)
        for j in range(GROUP):
            rows = total[j * all_frames : (j + 1) * all_frames]
            scatter_position(spread, i * GROUP + j, positions, rows)
        return carry

    lax.fori_loop(0, positions // GROUP, step, 0)
    gather_frames(spread, grad_normed)


def project_kernel(attended, w_out, projected, spread):
    positions, frames, channels = attended.shape

    def step(i, carry):
        rows = attended[pl.ds(i * GROUP, GROUP)].reshape(GROUP * frames, channels)
        total = dot(rows, w_out[...]).astype(BF16).astype(F32)
        for j in range(GROUP):
            part = total[j * frames : (j + 1) * frames]
            scatter_position(spread, i * GROUP + j, positions, part)
        return carry

    lax.fori_loop(0, positions // GROUP, step, 0)
    gather_frames(spread, projected)


def encode_kernel(frame_count, row_count, hidden, projected, encoded):
    frames_here = frame_count[lax.axis_index("tm")]
    rows_here = row_count[lax.axis_index("space")]
    frames, slots, columns, channels = encoded.shape
    tokens = slots * columns

    def step(frame, carry):
        total = hidden[:, frame].astype(F32) + projected[:, frame].astype(F32)
        total = total.reshape(tokens, channels)
        used = token_mask(frame, frames_here, rows_here, columns, total.shape)
        total = jnp.where(used, total, 0.0).astype(BF16)
        encoded[frame] = total.reshape(slots, columns, channels)
        return carry

    lax.fori_loop(0, frames, step, 0)


def grad_hidden_kernel(
    frame_count, row_count, cotangent, hidden, grad_normed, grad_hidden, head, tail
):
    frames_here = frame_count[lax.axis_index("tm")]
    rows_here = row_count[lax.axis_index("space")]
    frames, slots, columns, channels = cotangent.shape
    tokens = slots * columns

    def step(frame, carry):
        hid = hidden[:, frame].astype(F32).reshape(tokens, channels)
        grad = grad_normed[:, frame].astype(F32).reshape(tokens, channels)
        outer = cotangent[frame].astype(F32).reshape(tokens, channels)
        inv = inverse_rms(hid)
        inner = jnp.mean(grad * hid, axis=-1, keepdims=True)
        total = outer + inv * grad - (inv * inv * inv * inner) * hid
        used = token_mask(frame, frames_here, rows_here, columns, total.shape)
        total = jnp.where(used, total, 0.0).astype(BF16)
        grad_hidden[frame] = total.reshape(slots, columns, channels)
        return carry

    lax.fori_loop(0, frames, step, 0)
    head[...] = grad_hidden[:, 0]
    tail[...] = grad_hidden[:, rows_here - 1]


def video_grad_kernel(frame_count, row_count, field, above, below, weight, out, extended):
    frames_here = frame_count[lax.axis_index("tm")]
    rows_here = row_count[lax.axis_index("space")]
    frames, slots, columns, channels = field.shape
    tokens = slots * columns
    fill_halo(extended, field, above, below, rows_here)

    def step(frame, carry):
        total = convolve_frame(extended, weight, frame, True)
        used = token_mask(frame, frames_here, rows_here, columns, total.shape)
        center = field[frame].reshape(tokens, channels).astype(F32)
        total = jnp.where(used, center + total, 0.0).astype(BF16)
        out[frame] = total.reshape(slots, columns, channels)
        return carry

    lax.fori_loop(0, frames, step, 0)


def share_rows(head, tail):
    ends = lax.axis_size("space") - 1
    above = lax.ppermute(tail, "space", [(i, i + 1) for i in range(ends)])
    below = lax.ppermute(head, "space", [(i + 1, i) for i in range(ends)])
    return above, below


def exchange(blocks):
    return lax.all_to_all(blocks, "tm", split_axis=0, concat_axis=0, tiled=True)


def body(video, cotangent, frame_count, row_count, w_conv, w_query, w_key, w_value, w_out):
    frames, slots, columns, channels = video.shape
    blocks = lax.axis_size("tm")
    positions = slots * columns // blocks
    all_frames = frames * blocks
    shaped = jax.ShapeDtypeStruct
    home = (frames, slots, columns, channels)
    sent = (blocks, frames, positions, channels)
    spread = (all_frames, positions, channels)
    ordered = (positions, all_frames, channels)
    edge = (frames, columns, channels)
    padded = (frames, slots + 2, columns, channels)
    size = 2 * frames * slots * columns * channels
    product = 2 * frames * slots * columns * channels * channels
    inner = 2 * positions * all_frames * all_frames * channels

    outgoing = cotangent.reshape(frames, blocks, positions, channels).transpose(1, 0, 2, 3)
    grads_in = exchange(outgoing).reshape(spread)
    head, tail = pl.pallas_call(
        edges_kernel,
        out_shape=[shaped(edge, BF16)] * 2,
        in_specs=specs(SMEM, pl.ANY),
        out_specs=specs(VMEM, VMEM),
        scratch_shapes=[pltpu.SemaphoreType.DMA((2,))],
        cost_estimate=cost(0, size // 2),
        name="edges",
    )(row_count, video)
    above, below = share_rows(head, tail)
    hidden, normed = pl.pallas_call(
        hidden_kernel,
        out_shape=[shaped(sent, BF16)] * 2,
        in_specs=specs(SMEM, SMEM, VMEM, VMEM, VMEM, VMEM),
        out_specs=specs(VMEM, VMEM),
        scratch_shapes=[VMEM(padded, BF16)],
        cost_estimate=cost(9 * product, 4 * size),
        name="hidden",
    )(frame_count, row_count, video, above, below, w_conv)
    slot = lax.broadcasted_iota(jnp.int32, (blocks, frames, all_frames), 1)
    used = (slot < frame_count[:, None, None]).astype(F32).reshape(all_frames, all_frames)
    grads = pl.pallas_call(
        grads_kernel,
        out_shape=shaped(ordered, BF16),
        in_specs=specs(VMEM, VMEM, VMEM),
        out_specs=pl.BlockSpec(memory_space=VMEM),
        scratch_shapes=[VMEM((channels // LANES, all_frames * positions, LANES), F32), VMEM(ordered, BF16)],
        cost_estimate=cost(product, 2 * size),
        name="grads",
    )(grads_in, used, w_out)
    normed_in = exchange(normed).reshape(spread)
    group = (GROUP * all_frames, channels)
    attended, grad_normed = pl.pallas_call(
        attention_kernel,
        out_shape=[shaped(ordered, BF16), shaped(spread, BF16)],
        in_specs=specs(*[VMEM] * 6),
        out_specs=specs(VMEM, VMEM),
        scratch_shapes=[VMEM((channels // LANES, all_frames * positions, LANES), F32), VMEM(ordered, BF16)]
        + [VMEM(group, BF16)] * 6,
        cost_estimate=cost(6 * product + 6 * inner, 4 * size),
        name="attention",
    )(normed_in, grads, used, w_query, w_key, w_value)
    grad_home = exchange(grad_normed.reshape(sent))
    projected = pl.pallas_call(
        project_kernel,
        out_shape=shaped(spread, BF16),
        in_specs=specs(VMEM, VMEM),
        out_specs=pl.BlockSpec(memory_space=VMEM),
        scratch_shapes=[VMEM((channels // LANES, all_frames * positions, LANES), F32)],
        cost_estimate=cost(product, 2 * size),
        name="project",
    )(attended, w_out)
    grad_hidden, head, tail = pl.pallas_call(
        grad_hidden_kernel,
        out_shape=[shaped(home, BF16), shaped(edge, BF16), shaped(edge, BF16)],
        in_specs=specs(SMEM, SMEM, VMEM, VMEM, VMEM),
        out_specs=specs(VMEM, VMEM, VMEM),
        cost_estimate=cost(0, 5 * size),
        name="grad_hidden",
    )(frame_count, row_count, cotangent, hidden, grad_home)
    projected_home = exchange(projected.reshape(sent))
    above, below = share_rows(head, tail)
    video_grad = pl.pallas_call(
        video_grad_kernel,
        out_shape=shaped(home, BF16),
        in_specs=specs(SMEM, SMEM, VMEM, VMEM, VMEM, VMEM),
        out_specs=pl.BlockSpec(memory_space=VMEM),
        scratch_shapes=[VMEM(padded, BF16)],
        cost_estimate=cost(9 * product, 3 * size),
        name="video_grad",
    )(frame_count, row_count, grad_hidden, above, below, w_conv)
    encoded = pl.pallas_call(
        encode_kernel,
        out_shape=shaped(home, BF16),
        in_specs=specs(SMEM, SMEM, VMEM, VMEM),
        out_specs=pl.BlockSpec(memory_space=VMEM),
        cost_estimate=cost(0, 3 * size),
        name="encode",
    )(frame_count, row_count, hidden, projected_home)
    return encoded, video_grad


def solution(mesh):
    field = P("tm", "space", None, None)
    in_specs = (field, field) + (P(),) * 7
    return jax.shard_map(
        body, mesh=mesh, in_specs=in_specs, out_specs=(field, field), check_vma=False
    )
```

```python
import jax
import jax.numpy as jnp
from jax import lax
from jax.experimental import pallas as pl
from jax.experimental.pallas import tpu as pltpu
from jax.sharding import PartitionSpec as P


BF16 = jnp.bfloat16
F32 = jnp.float32
GROUP = 4
LANES = 128
VMEM = pltpu.VMEM
SMEM = pltpu.SMEM
HBM = pltpu.HBM
ON_CHIP = object()


def dot(a, b, contract=(1, 0)):
    return lax.dot_general(
        a, b, (((contract[0],), (contract[1],)), ((), ())), preferred_element_type=F32
    )


def specs(*spaces):
    return [pl.BlockSpec(memory_space=space) for space in spaces]


def cost(flops, moved):
    return pl.CostEstimate(flops=flops, bytes_accessed=moved, transcendentals=0)


def edges_kernel(row_count, field, head, tail, sems):
    rows_here = row_count[lax.axis_index("space")]
    first = pltpu.make_async_copy(field.at[:, 0], head, sems.at[0])
    last = pltpu.make_async_copy(field.at[:, rows_here - 1], tail, sems.at[1])
    first.start()
    last.start()
    first.wait()
    last.wait()


def fill_halo(extended, field, above, below, rows_here):
    slots = field.shape[1]
    extended[:, 1 : 1 + slots] = field[...]
    extended[:, 0] = above[...]
    extended[:, 1 + rows_here] = below[...]


def convolve_frame(extended, weight, frame, flipped):
    _, padded, columns, channels = extended.shape
    tokens = (padded - 2) * columns
    column = lax.broadcasted_iota(jnp.int32, (tokens, channels), 0) % columns
    total = None
    for b in range(3):
        part = None
        for a in range(3):
            view = extended[frame, a : a + padded - 2].reshape(tokens, channels)
            if flipped:
                term = dot(view, weight[2 - a, 2 - b], (1, 1))
            else:
                term = dot(view, weight[a, b])
            part = term if part is None else part + term
        if b == 0:
            part = jnp.where(column == 0, 0.0, pltpu.roll(part, 1, 0))
        elif b == 2:
            part = jnp.where(column == columns - 1, 0.0, pltpu.roll(part, tokens - 1, 0))
        total = part if total is None else total + part
    return total


def token_mask(frame, frames_here, rows_here, columns, shape):
    row = lax.broadcasted_iota(jnp.int32, shape, 0) // columns
    return (row < rows_here) & (frame < frames_here)


def inverse_rms(hidden):
    return lax.rsqrt(jnp.mean(hidden * hidden, axis=-1, keepdims=True) + 1e-06)


def hidden_kernel(
    frame_count, row_count, field, above, below, weight, hidden_out, normed_out, extended
):
    frames_here = frame_count[lax.axis_index("tm")]
    rows_here = row_count[lax.axis_index("space")]
    frames, slots, columns, channels = field.shape
    tokens = slots * columns
    fill_halo(extended, field, above, below, rows_here)

    def step(frame, carry):
        total = convolve_frame(extended, weight, frame, False)
        used = token_mask(frame, frames_here, rows_here, columns, total.shape)
        center = field[frame].reshape(tokens, channels).astype(F32)
        hidden = jnp.where(used, center + total, 0.0).astype(BF16)
        hidden_out[:, frame] = hidden.reshape(hidden_out.shape[0], -1, channels)
        hidden_f = hidden.astype(F32)
        normed = (hidden_f * inverse_rms(hidden_f)).astype(BF16)
        normed_out[:, frame] = normed.reshape(normed_out.shape[0], -1, channels)
        return carry

    lax.fori_loop(0, frames, step, 0)


def load_position(spread, position, positions, scale=None):
    parts = []
    for h in range(spread.shape[0]):
        rows = spread[h, pl.ds(position, spread.shape[1] // positions, stride=positions), :]
        parts.append((rows if scale is None else rows * scale).astype(BF16))
    return jnp.concatenate(parts, axis=1)


def store_position(spread, position, positions, rows):
    for h in range(spread.shape[0]):
        part = rows[:, h * LANES : (h + 1) * LANES]
        spread[h, pl.ds(position, rows.shape[0], stride=positions), :] = part


def widen(source, spread):
    for h in range(spread.shape[0]):
        part = source[:, :, h * LANES : (h + 1) * LANES].astype(F32)
        spread[h] = part.reshape(spread.shape[1], LANES)


def narrow(spread, held, target, sems):
    frames, positions, _ = held.shape
    pieces = 4
    size = frames // pieces
    copies = []
    for i in range(pieces):
        here = slice(i * size, (i + 1) * size)
        for h in range(spread.shape[0]):
            part = spread[h, i * size * positions : (i + 1) * size * positions]
            part = part.reshape(size, positions, LANES)
            held[here, :, h * LANES : (h + 1) * LANES] = part.astype(BF16)
        copy = pltpu.make_async_copy(held.at[here], target.at[here], sems.at[i])
        copy.start()
        copies.append(copy)
    for copy in copies:
        copy.wait()


def send_kernel(field, out, held, sems):
    frames = field.shape[0]
    arrive = [
        pltpu.make_async_copy(field.at[f], held.at[f], sems.at[0, f]) for f in range(frames)
    ]
    leave = [
        pltpu.make_async_copy(held.at[f], out.at[:, f], sems.at[1, f]) for f in range(frames)
    ]
    for copy in arrive:
        copy.start()
    for f in range(frames):
        arrive[f].wait()
        leave[f].start()
    for copy in leave:
        copy.wait()


def grads_kernel(cotangent, used, w_out, grad_out, spread, ordered):
    all_frames, positions, channels = cotangent.shape
    widen(cotangent, spread)
    for first in range(0, positions, GROUP):
        for p in range(first, first + GROUP):
            here = slice(p * all_frames, (p + 1) * all_frames)
            ordered[here] = load_position(spread, p, positions, used[...])
        here = slice(first * all_frames, (first + GROUP) * all_frames)
        grads = dot(ordered[here], w_out[...], (1, 1)).astype(BF16)
        grad_out[first : first + GROUP] = grads.reshape(GROUP, all_frames, channels)


def softmax_probs(query, key, allowed, scale):
    scores = jnp.where(allowed, dot(key, query, (1, 1)) * scale, -1e30)
    expo = jnp.exp(scores - jnp.max(scores, axis=0, keepdims=True))
    return expo * (1.0 / jnp.sum(expo, axis=0, keepdims=True))


def allowed_pairs(used):
    tile = (used.shape[0], used.shape[0])
    source = lax.broadcasted_iota(jnp.int32, tile, 0)
    reader = lax.broadcasted_iota(jnp.int32, tile, 1)
    return (source <= reader) & (used[...] > 0.0)


def attention_kernel(
    normed, grads_in, used, w_query, w_key, w_value, grad_normed, kept,
    grads, weights, spread, result, out, ordered, query_s, key_s, value_s, dq_s, dk_s, dv_s, sems,
):
    loads = [
        pltpu.make_async_copy(w, weights.at[i], sems.at[i])
        for i, w in enumerate((w_query, w_key, w_value))
    ]
    loads.append(pltpu.make_async_copy(grads_in, grads, sems.at[3]))
    for copy in loads:
        copy.start()
    all_frames, positions, channels = normed.shape
    widen(normed, spread)
    allowed = allowed_pairs(used)
    scale = channels ** (-0.5)
    for copy in loads[:3]:
        copy.wait()
    keeps = []

    for first in range(0, positions, GROUP):
        group = slice(first * all_frames, (first + GROUP) * all_frames)
        for p in range(first, first + GROUP):
            ordered[p * all_frames : (p + 1) * all_frames] = load_position(spread, p, positions)
        rows = ordered[group]
        keep = pltpu.make_async_copy(
            ordered.at[group], kept.at[group], sems.at[4 + first // GROUP]
        )
        keep.start()
        keeps.append(keep)
        query_s[group] = dot(rows, weights[0]).astype(BF16)
        key_s[group] = dot(rows, weights[1]).astype(BF16)
        value_s[group] = dot(rows, weights[2]).astype(BF16)
        if first == 0:
            loads[3].wait()
        for p in range(first, first + GROUP):
            here = slice(p * all_frames, (p + 1) * all_frames)
            query, key, value, grad = query_s[here], key_s[here], value_s[here], grads[p]
            probs = softmax_probs(query, key, allowed, scale)
            low = probs.astype(BF16)
            grad_probs = dot(value, grad, (1, 1))
            delta = jnp.sum(low.astype(F32) * grad_probs, axis=0, keepdims=True)
            grad_scores = (probs * (grad_probs - delta) * scale).astype(BF16)
            dv_s[here] = dot(low, grad).astype(BF16)
            dk_s[here] = dot(grad_scores, query).astype(BF16)
            dq_s[here] = dot(grad_scores, key, (0, 0)).astype(BF16)
        total = dot(dq_s[group], weights[0], (1, 1))
        total = total + dot(dk_s[group], weights[1], (1, 1))
        total = total + dot(dv_s[group], weights[2], (1, 1))
        total = total.astype(BF16).astype(F32)
        for j in range(GROUP):
            part = total[j * all_frames : (j + 1) * all_frames]
            store_position(result, first + j, positions, part)
    narrow(result, out, grad_normed, sems)
    for copy in keeps:
        copy.wait()


def project_kernel(
    ordered, used, w_query, w_key, w_value, w_out, projected,
    spread, query_s, key_s, value_s, attended,
):
    all_frames, positions, channels = projected.shape
    allowed = allowed_pairs(used)
    scale = channels ** (-0.5)

    def step(i, carry):
        first = pl.multiple_of(i * GROUP * all_frames, GROUP * all_frames)
        rows = ordered[pl.ds(first, GROUP * all_frames)]
        query_s[...] = dot(rows, w_query[...]).astype(BF16)
        key_s[...] = dot(rows, w_key[...]).astype(BF16)
        value_s[...] = dot(rows, w_value[...]).astype(BF16)
        for j in range(GROUP):
            here = slice(j * all_frames, (j + 1) * all_frames)
            low = softmax_probs(query_s[here], key_s[here], allowed, scale).astype(BF16)
            attended[here] = dot(low, value_s[here], (0, 0)).astype(BF16)
        total = dot(attended[...], w_out[...]).astype(BF16).astype(F32)
        for j in range(GROUP):
            part = total[j * all_frames : (j + 1) * all_frames]
            store_position(spread, i * GROUP + j, positions, part)
        return carry

    lax.fori_loop(0, positions // GROUP, step, 0)
    for h in range(spread.shape[0]):
        part = spread[h].reshape(all_frames, positions, LANES)
        projected[:, :, h * LANES : (h + 1) * LANES] = part.astype(BF16)


def encode_kernel(frame_count, row_count, hidden, projected, encoded, held, sems):
    frames_here = frame_count[lax.axis_index("tm")]
    rows_here = row_count[lax.axis_index("space")]
    frames, slots, columns, channels = encoded.shape
    tokens = slots * columns
    copies = []
    for frame in range(frames):
        total = hidden[:, frame].astype(F32) + projected[:, frame].astype(F32)
        total = total.reshape(tokens, channels)
        used = token_mask(frame, frames_here, rows_here, columns, total.shape)
        total = jnp.where(used, total, 0.0).astype(BF16)
        held[frame] = total.reshape(slots, columns, channels)
        copy = pltpu.make_async_copy(held.at[frame], encoded.at[frame], sems.at[frame])
        copy.start()
        copies.append(copy)
    for copy in copies:
        copy.wait()


def grad_hidden_kernel(
    frame_count, row_count, cotangent, hidden, grad_normed, grad_hidden, head, tail
):
    frames_here = frame_count[lax.axis_index("tm")]
    rows_here = row_count[lax.axis_index("space")]
    frames, slots, columns, channels = cotangent.shape
    tokens = slots * columns

    def step(frame, carry):
        hid = hidden[:, frame].astype(F32).reshape(tokens, channels)
        grad = grad_normed[:, frame].astype(F32).reshape(tokens, channels)
        outer = cotangent[frame].astype(F32).reshape(tokens, channels)
        inv = inverse_rms(hid)
        inner = jnp.mean(grad * hid, axis=-1, keepdims=True)
        total = outer + inv * grad - (inv * inv * inv * inner) * hid
        used = token_mask(frame, frames_here, rows_here, columns, total.shape)
        total = jnp.where(used, total, 0.0).astype(BF16)
        grad_hidden[frame] = total.reshape(slots, columns, channels)
        return carry

    lax.fori_loop(0, frames, step, 0)
    head[...] = grad_hidden[:, 0]
    tail[...] = grad_hidden[:, rows_here - 1]


def video_grad_kernel(frame_count, row_count, field, above, below, weight, out, extended):
    frames_here = frame_count[lax.axis_index("tm")]
    rows_here = row_count[lax.axis_index("space")]
    frames, slots, columns, channels = field.shape
    tokens = slots * columns
    fill_halo(extended, field, above, below, rows_here)

    def step(frame, carry):
        total = convolve_frame(extended, weight, frame, True)
        used = token_mask(frame, frames_here, rows_here, columns, total.shape)
        center = field[frame].reshape(tokens, channels).astype(F32)
        total = jnp.where(used, center + total, 0.0).astype(BF16)
        out[frame] = total.reshape(slots, columns, channels)
        return carry

    lax.fori_loop(0, frames, step, 0)


def share_rows(head, tail):
    ends = lax.axis_size("space") - 1
    above = lax.ppermute(tail, "space", [(i, i + 1) for i in range(ends)])
    below = lax.ppermute(head, "space", [(i + 1, i) for i in range(ends)])
    return above, below


def exchange(blocks):
    return lax.all_to_all(blocks, "tm", split_axis=0, concat_axis=0, tiled=True)


def body(video, cotangent, frame_count, row_count, w_conv, w_query, w_key, w_value, w_out):
    frames, slots, columns, channels = video.shape
    blocks = lax.axis_size("tm")
    positions = slots * columns // blocks
    all_frames = frames * blocks
    shaped = jax.ShapeDtypeStruct
    home = (frames, slots, columns, channels)
    sent = (blocks, frames, positions, channels)
    spread = (all_frames, positions, channels)
    ordered = (positions, all_frames, channels)
    edge = (frames, columns, channels)
    padded = (frames, slots + 2, columns, channels)
    size = 2 * frames * slots * columns * channels
    product = 2 * frames * slots * columns * channels * channels
    inner = 2 * positions * all_frames * all_frames * channels

    def call(kernel, outs, ins, args, scratch, flops, moved, out_spaces=None):
        args = [
            pltpu.with_memory_space_constraint(x, VMEM) if space is ON_CHIP else x
            for x, space in zip(args, ins)
        ]
        ins = [VMEM if space is ON_CHIP else space for space in ins]
        return pl.pallas_call(
            kernel,
            out_shape=outs,
            in_specs=specs(*ins),
            out_specs=specs(*(out_spaces or [VMEM] * len(outs))),
            scratch_shapes=scratch,
            cost_estimate=cost(flops, moved),
        )(*args)

    dma = pltpu.SemaphoreType.DMA
    wide = VMEM((channels // LANES, all_frames * positions, LANES), F32)
    flat = VMEM((all_frames * positions, channels), BF16)
    part = VMEM((GROUP * all_frames, channels), BF16)
    chunked = (frames, blocks, positions, channels)

    (outgoing,) = call(
        send_kernel, [shaped(sent, BF16)], [HBM], [cotangent.reshape(chunked)],
        [VMEM(chunked, BF16), dma((2, frames))], 0, size, [HBM],
    )
    grads_in = exchange(outgoing).reshape(spread)
    head, tail = call(
        edges_kernel, [VMEM(edge, BF16)] * 2, [SMEM, HBM], [row_count, video],
        [dma((2,))], 0, size // 4,
    )
    above, below = share_rows(head, tail)
    hidden, normed = call(
        hidden_kernel, [shaped(sent, BF16)] * 2, [SMEM, SMEM, VMEM, ON_CHIP, ON_CHIP, VMEM],
        [frame_count, row_count, video, above, below, w_conv], [VMEM(padded, BF16)],
        9 * product, 4 * size,
    )
    normed_in = exchange(normed).reshape(spread)
    slot = lax.broadcasted_iota(jnp.int32, (blocks, frames, LANES), 1)
    used = (slot < frame_count[:, None, None]).astype(F32).reshape(all_frames, LANES)
    (grads,) = call(
        grads_kernel, [shaped(ordered, BF16)], [ON_CHIP, ON_CHIP, VMEM], [grads_in, used, w_out],
        [wide, flat], product, 2 * size,
    )
    grad_normed, kept = call(
        attention_kernel,
        [shaped(spread, BF16), shaped((all_frames * positions, channels), BF16)],
        [ON_CHIP, HBM, ON_CHIP, HBM, HBM, HBM],
        [normed_in, grads, used, w_query, w_key, w_value],
        [VMEM(ordered, BF16), VMEM((3, channels, channels), BF16), wide, wide, VMEM(spread, BF16)]
        + [flat] * 7 + [dma((4 + positions // GROUP,))],
        6 * product + 5 * inner, 4 * size, [HBM, HBM],
    )
    grad_home = exchange(grad_normed.reshape(sent))
    (projected,) = call(
        project_kernel, [shaped(spread, BF16)], [VMEM, ON_CHIP] + [VMEM] * 4,
        [kept, used, w_query, w_key, w_value, w_out],
        [wide] + [part] * 4, 4 * product + 2 * inner, 2 * size,
    )
    projected_home = exchange(projected.reshape(sent))
    grad_hidden, head, tail = call(
        grad_hidden_kernel, [shaped(home, BF16), shaped(edge, BF16), shaped(edge, BF16)],
        [SMEM, SMEM, VMEM, VMEM, ON_CHIP],
        [frame_count, row_count, cotangent, hidden, grad_home], [], 0, 5 * size,
    )
    above, below = share_rows(head, tail)
    (video_grad,) = call(
        video_grad_kernel, [shaped(home, BF16)], [SMEM, SMEM, VMEM, ON_CHIP, ON_CHIP, VMEM],
        [frame_count, row_count, grad_hidden, above, below, w_conv], [VMEM(padded, BF16)],
        9 * product, 3 * size,
    )
    (encoded,) = call(
        encode_kernel, [shaped(home, BF16)], [SMEM, SMEM, ON_CHIP, ON_CHIP],
        [frame_count, row_count, hidden, projected_home],
        [VMEM(home, BF16), dma((frames,))], 0, 3 * size, [HBM],
    )
    return encoded, video_grad


def solution(mesh):
    field = P("tm", "space", None, None)
    in_specs = (field, field) + (P(),) * 7

    return jax.shard_map(
        body, mesh=mesh, in_specs=in_specs, out_specs=(field, field), check_vma=False
    )
```

```python
import jax
import jax.numpy as jnp
from jax import lax
from jax.experimental import pallas as pl
from jax.experimental.pallas import tpu as pltpu
from jax.sharding import PartitionSpec as P


BF16 = jnp.bfloat16
F32 = jnp.float32
GROUP = 4
LANES = 128
VMEM = pltpu.VMEM
SMEM = pltpu.SMEM
HBM = pltpu.HBM
ON_CHIP = object()


def dot(a, b, contract=(1, 0)):
    return lax.dot_general(
        a, b, (((contract[0],), (contract[1],)), ((), ())), preferred_element_type=F32
    )


def specs(*spaces):
    return [pl.BlockSpec(memory_space=space) for space in spaces]


def cost(flops, moved):
    return pl.CostEstimate(flops=flops, bytes_accessed=moved, transcendentals=0)


def edges_kernel(row_count, field, head, tail, sems):
    rows_here = row_count[lax.axis_index("space")]
    first = pltpu.make_async_copy(field.at[:, 0], head, sems.at[0])
    last = pltpu.make_async_copy(field.at[:, rows_here - 1], tail, sems.at[1])
    first.start()
    last.start()
    first.wait()
    last.wait()


def fill_halo(extended, field, above, below, rows_here):
    slots = field.shape[1]
    extended[:, 1 : 1 + slots] = field[...]
    extended[:, 0] = above[...]
    extended[:, 1 + rows_here] = below[...]


def convolve_frame(extended, weight, frame, flipped):
    _, padded, columns, channels = extended.shape
    tokens = (padded - 2) * columns
    column = lax.broadcasted_iota(jnp.int32, (tokens, channels), 0) % columns
    total = None
    for b in range(3):
        part = None
        for a in range(3):
            view = extended[frame, a : a + padded - 2].reshape(tokens, channels)
            if flipped:
                term = dot(view, weight[2 - a, 2 - b], (1, 1))
            else:
                term = dot(view, weight[a, b])
            part = term if part is None else part + term
        if b == 0:
            part = jnp.where(column == 0, 0.0, pltpu.roll(part, 1, 0))
        elif b == 2:
            part = jnp.where(column == columns - 1, 0.0, pltpu.roll(part, tokens - 1, 0))
        total = part if total is None else total + part
    return total


def token_mask(frame, frames_here, rows_here, columns, shape):
    row = lax.broadcasted_iota(jnp.int32, shape, 0) // columns
    return (row < rows_here) & (frame < frames_here)


def inverse_rms(hidden):
    return lax.rsqrt(jnp.mean(hidden * hidden, axis=-1, keepdims=True) + 1e-06)


def hidden_kernel(
    frame_count, row_count, field, above, below, weight, hidden_out, normed_out, extended
):
    frames_here = frame_count[lax.axis_index("tm")]
    rows_here = row_count[lax.axis_index("space")]
    frames, slots, columns, channels = field.shape
    tokens = slots * columns
    fill_halo(extended, field, above, below, rows_here)

    def step(frame, carry):
        total = convolve_frame(extended, weight, frame, False)
        used = token_mask(frame, frames_here, rows_here, columns, total.shape)
        center = field[frame].reshape(tokens, channels).astype(F32)
        hidden = jnp.where(used, center + total, 0.0).astype(BF16)
        hidden_out[:, frame] = hidden.reshape(hidden_out.shape[0], -1, channels)
        hidden_f = hidden.astype(F32)
        normed = (hidden_f * inverse_rms(hidden_f)).astype(BF16)
        normed_out[:, frame] = normed.reshape(normed_out.shape[0], -1, channels)
        return carry

    lax.fori_loop(0, frames, step, 0)


def load_position(spread, position, positions, scale=None):
    parts = []
    for h in range(spread.shape[0]):
        rows = spread[h, pl.ds(position, spread.shape[1] // positions, stride=positions), :]
        parts.append((rows if scale is None else rows * scale).astype(BF16))
    return jnp.concatenate(parts, axis=1)


def store_position(spread, position, positions, rows):
    for h in range(spread.shape[0]):
        part = rows[:, h * LANES : (h + 1) * LANES]
        spread[h, pl.ds(position, rows.shape[0], stride=positions), :] = part


def widen(source, spread):
    for h in range(spread.shape[0]):
        part = source[:, :, h * LANES : (h + 1) * LANES].astype(F32)
        spread[h] = part.reshape(spread.shape[1], LANES)


def narrow(spread, held, target, sems):
    frames, positions, _ = held.shape
    pieces = 4
    size = frames // pieces
    copies = []
    for i in range(pieces):
        here = slice(i * size, (i + 1) * size)
        for h in range(spread.shape[0]):
            part = spread[h, i * size * positions : (i + 1) * size * positions]
            part = part.reshape(size, positions, LANES)
            held[here, :, h * LANES : (h + 1) * LANES] = part.astype(BF16)
        copy = pltpu.make_async_copy(held.at[here], target.at[here], sems.at[i])
        copy.start()
        copies.append(copy)
    for copy in copies:
        copy.wait()


def send_kernel(field, out, held, sems):
    frames = field.shape[0]
    arrive = [
        pltpu.make_async_copy(field.at[f], held.at[f], sems.at[0, f]) for f in range(frames)
    ]
    leave = [
        pltpu.make_async_copy(held.at[f], out.at[:, f], sems.at[1, f]) for f in range(frames)
    ]
    for copy in arrive:
        copy.start()
    for f in range(frames):
        arrive[f].wait()
        leave[f].start()
    for copy in leave:
        copy.wait()


def grads_kernel(cotangent, used, w_out, grad_out, spread, ordered):
    all_frames, positions, channels = cotangent.shape
    widen(cotangent, spread)
    for first in range(0, positions, GROUP):
        for p in range(first, first + GROUP):
            here = slice(p * all_frames, (p + 1) * all_frames)
            ordered[here] = load_position(spread, p, positions, used[...])
        here = slice(first * all_frames, (first + GROUP) * all_frames)
        grads = dot(ordered[here], w_out[...], (1, 1)).astype(BF16)
        grad_out[first : first + GROUP] = grads.reshape(GROUP, all_frames, channels)


def softmax_probs(query, key, allowed, scale):
    scores = jnp.where(allowed, dot(key, query, (1, 1)) * scale, -1e30)
    expo = jnp.exp(scores - jnp.max(scores, axis=0, keepdims=True))
    return expo * (1.0 / jnp.sum(expo, axis=0, keepdims=True))


def allowed_pairs(used):
    tile = (used.shape[0], used.shape[0])
    source = lax.broadcasted_iota(jnp.int32, tile, 0)
    reader = lax.broadcasted_iota(jnp.int32, tile, 1)
    return (source <= reader) & (used[...] > 0.0)


def attention_kernel(
    normed, grads_in, used, w_query, w_key, w_value, grad_normed, kept,
    grads, weights, bias, spread, result, out, ordered, fields, scores, grad_probs,
    probs_low, grad_scores, backs, sems,
):
    all_frames, positions, channels = normed.shape
    loads = [
        pltpu.make_async_copy(w, weights.at[:, i * channels : (i + 1) * channels], sems.at[i])
        for i, w in enumerate((w_query, w_key, w_value))
    ]
    loads.append(pltpu.make_async_copy(grads_in, grads, sems.at[3]))
    for copy in loads:
        copy.start()
    widen(normed, spread)
    scale = channels ** (-0.5)
    bias[...] = jnp.where(allowed_pairs(used), 0.0, -1e30)
    keeps = []

    def rows_of(p):
        return slice(p * all_frames, (p + 1) * all_frames)

    def lanes_of(i):
        return slice(i * channels, (i + 1) * channels)

    def project_group(first):
        group = slice(first * all_frames, (first + GROUP) * all_frames)
        for p in range(first, first + GROUP):
            ordered[rows_of(p)] = load_position(spread, p, positions)
        keep = pltpu.make_async_copy(
            ordered.at[group], kept.at[group], sems.at[4 + first // GROUP]
        )
        keep.start()
        keeps.append(keep)
        for i in range(3):
            product = dot(ordered[group], weights[:, lanes_of(i)])
            fields[group, lanes_of(i)] = product.astype(BF16)

    def pair_products(p):
        here = rows_of(p)
        scores[p] = dot(fields[here, lanes_of(1)], fields[here, lanes_of(0)], (1, 1))
        grad_probs[p] = dot(fields[here, lanes_of(2)], grads[p], (1, 1))

    def softmax(p):
        logits = scores[p] * scale + bias[...]
        expo = jnp.exp(logits - jnp.max(logits, axis=0, keepdims=True))
        probs = expo * (1.0 / jnp.sum(expo, axis=0, keepdims=True))
        low = probs.astype(BF16)
        probs_low[p] = low
        grad = grad_probs[p]
        delta = jnp.sum(low.astype(F32) * grad, axis=0, keepdims=True)
        grad_scores[p] = (probs * (grad - delta) * scale).astype(BF16)

    def back_products(p):
        here = rows_of(p)
        backs[here, lanes_of(0)] = dot(
            grad_scores[p], fields[here, lanes_of(1)], (0, 0)
        ).astype(BF16)
        backs[here, lanes_of(1)] = dot(grad_scores[p], fields[here, lanes_of(0)]).astype(BF16)
        backs[here, lanes_of(2)] = dot(probs_low[p], grads[p]).astype(BF16)

    def back_group(first):
        group = slice(first * all_frames, (first + GROUP) * all_frames)
        total = dot(backs[group], weights[...], (1, 1)).astype(BF16).astype(F32)
        for j in range(GROUP):
            part = total[j * all_frames : (j + 1) * all_frames]
            store_position(result, first + j, positions, part)

    for copy in loads[:3]:
        copy.wait()
    project_group(0)
    loads[3].wait()
    for first in range(0, positions, GROUP):
        group = range(first, first + GROUP)
        for p in group:
            pair_products(p)
        if first + GROUP < positions:
            project_group(first + GROUP)
        for p in group:
            softmax(p)
        if first > 0:
            back_group(first - GROUP)
        for p in group:
            back_products(p)
    back_group(positions - GROUP)
    narrow(result, out, grad_normed, sems)
    for copy in keeps:
        copy.wait()


def project_kernel(
    ordered, used, w_query, w_key, w_value, w_out, projected,
    spread, query_s, key_s, value_s, attended,
):
    all_frames, positions, channels = projected.shape
    allowed = allowed_pairs(used)
    scale = channels ** (-0.5)

    def step(i, carry):
        first = pl.multiple_of(i * GROUP * all_frames, GROUP * all_frames)
        rows = ordered[pl.ds(first, GROUP * all_frames)]
        query_s[...] = dot(rows, w_query[...]).astype(BF16)
        key_s[...] = dot(rows, w_key[...]).astype(BF16)
        value_s[...] = dot(rows, w_value[...]).astype(BF16)
        for j in range(GROUP):
            here = slice(j * all_frames, (j + 1) * all_frames)
            low = softmax_probs(query_s[here], key_s[here], allowed, scale).astype(BF16)
            attended[here] = dot(low, value_s[here], (0, 0)).astype(BF16)
        total = dot(attended[...], w_out[...]).astype(BF16).astype(F32)
        for j in range(GROUP):
            part = total[j * all_frames : (j + 1) * all_frames]
            store_position(spread, i * GROUP + j, positions, part)
        return carry

    lax.fori_loop(0, positions // GROUP, step, 0)
    for h in range(spread.shape[0]):
        part = spread[h].reshape(all_frames, positions, LANES)
        projected[:, :, h * LANES : (h + 1) * LANES] = part.astype(BF16)


def encode_kernel(frame_count, row_count, hidden, projected, encoded, held, sems):
    frames_here = frame_count[lax.axis_index("tm")]
    rows_here = row_count[lax.axis_index("space")]
    frames, slots, columns, channels = encoded.shape
    tokens = slots * columns
    copies = []
    for frame in range(frames):
        total = hidden[:, frame].astype(F32) + projected[:, frame].astype(F32)
        total = total.reshape(tokens, channels)
        used = token_mask(frame, frames_here, rows_here, columns, total.shape)
        total = jnp.where(used, total, 0.0).astype(BF16)
        held[frame] = total.reshape(slots, columns, channels)
        copy = pltpu.make_async_copy(held.at[frame], encoded.at[frame], sems.at[frame])
        copy.start()
        copies.append(copy)
    for copy in copies:
        copy.wait()


def grad_hidden_kernel(
    frame_count, row_count, cotangent, hidden, grad_normed, grad_hidden, head, tail
):
    frames_here = frame_count[lax.axis_index("tm")]
    rows_here = row_count[lax.axis_index("space")]
    frames, slots, columns, channels = cotangent.shape
    tokens = slots * columns

    def step(frame, carry):
        hid = hidden[:, frame].astype(F32).reshape(tokens, channels)
        grad = grad_normed[:, frame].astype(F32).reshape(tokens, channels)
        outer = cotangent[frame].astype(F32).reshape(tokens, channels)
        inv = inverse_rms(hid)
        inner = jnp.mean(grad * hid, axis=-1, keepdims=True)
        total = outer + inv * grad - (inv * inv * inv * inner) * hid
        used = token_mask(frame, frames_here, rows_here, columns, total.shape)
        total = jnp.where(used, total, 0.0).astype(BF16)
        grad_hidden[frame] = total.reshape(slots, columns, channels)
        return carry

    lax.fori_loop(0, frames, step, 0)
    head[...] = grad_hidden[:, 0]
    tail[...] = grad_hidden[:, rows_here - 1]


def video_grad_kernel(frame_count, row_count, field, above, below, weight, out, extended):
    frames_here = frame_count[lax.axis_index("tm")]
    rows_here = row_count[lax.axis_index("space")]
    frames, slots, columns, channels = field.shape
    tokens = slots * columns
    fill_halo(extended, field, above, below, rows_here)

    def step(frame, carry):
        total = convolve_frame(extended, weight, frame, True)
        used = token_mask(frame, frames_here, rows_here, columns, total.shape)
        center = field[frame].reshape(tokens, channels).astype(F32)
        total = jnp.where(used, center + total, 0.0).astype(BF16)
        out[frame] = total.reshape(slots, columns, channels)
        return carry

    lax.fori_loop(0, frames, step, 0)


def share_rows(head, tail):
    ends = lax.axis_size("space") - 1
    above = lax.ppermute(tail, "space", [(i, i + 1) for i in range(ends)])
    below = lax.ppermute(head, "space", [(i + 1, i) for i in range(ends)])
    return above, below


def exchange(blocks):
    return lax.all_to_all(blocks, "tm", split_axis=0, concat_axis=0, tiled=True)


def body(video, cotangent, frame_count, row_count, w_conv, w_query, w_key, w_value, w_out):
    frames, slots, columns, channels = video.shape
    blocks = lax.axis_size("tm")
    positions = slots * columns // blocks
    all_frames = frames * blocks
    shaped = jax.ShapeDtypeStruct
    home = (frames, slots, columns, channels)
    sent = (blocks, frames, positions, channels)
    spread = (all_frames, positions, channels)
    ordered = (positions, all_frames, channels)
    edge = (frames, columns, channels)
    padded = (frames, slots + 2, columns, channels)
    size = 2 * frames * slots * columns * channels
    product = 2 * frames * slots * columns * channels * channels
    inner = 2 * positions * all_frames * all_frames * channels

    def call(kernel, outs, ins, args, scratch, flops, moved, out_spaces=None):
        args = [
            pltpu.with_memory_space_constraint(x, VMEM) if space is ON_CHIP else x
            for x, space in zip(args, ins)
        ]
        ins = [VMEM if space is ON_CHIP else space for space in ins]
        return pl.pallas_call(
            kernel,
            out_shape=outs,
            in_specs=specs(*ins),
            out_specs=specs(*(out_spaces or [VMEM] * len(outs))),
            scratch_shapes=scratch,
            cost_estimate=cost(flops, moved),
        )(*args)

    dma = pltpu.SemaphoreType.DMA
    wide = VMEM((channels // LANES, all_frames * positions, LANES), F32)
    flat = VMEM((all_frames * positions, channels), BF16)
    part = VMEM((GROUP * all_frames, channels), BF16)
    triple = VMEM((all_frames * positions, 3 * channels), BF16)
    pairs = (all_frames, all_frames)
    chunked = (frames, blocks, positions, channels)

    (outgoing,) = call(
        send_kernel, [shaped(sent, BF16)], [HBM], [cotangent.reshape(chunked)],
        [VMEM(chunked, BF16), dma((2, frames))], 0, size, [HBM],
    )
    grads_in = exchange(outgoing).reshape(spread)
    head, tail = call(
        edges_kernel, [VMEM(edge, BF16)] * 2, [SMEM, HBM], [row_count, video],
        [dma((2,))], 0, size // 4,
    )
    above, below = share_rows(head, tail)
    hidden, normed = call(
        hidden_kernel, [shaped(sent, BF16)] * 2, [SMEM, SMEM, VMEM, ON_CHIP, ON_CHIP, VMEM],
        [frame_count, row_count, video, above, below, w_conv], [VMEM(padded, BF16)],
        9 * product, 4 * size,
    )
    normed_in = exchange(normed).reshape(spread)
    slot = lax.broadcasted_iota(jnp.int32, (blocks, frames, LANES), 1)
    used = (slot < frame_count[:, None, None]).astype(F32).reshape(all_frames, LANES)
    (grads,) = call(
        grads_kernel, [shaped(ordered, BF16)], [ON_CHIP, ON_CHIP, VMEM], [grads_in, used, w_out],
        [wide, flat], product, 2 * size,
    )
    grad_normed, kept = call(
        attention_kernel,
        [shaped(spread, BF16), shaped((all_frames * positions, channels), BF16)],
        [ON_CHIP, HBM, ON_CHIP, HBM, HBM, HBM],
        [normed_in, grads, used, w_query, w_key, w_value],
        [
            VMEM(ordered, BF16), VMEM((channels, 3 * channels), BF16), VMEM(pairs, F32), wide, wide,
            VMEM(spread, BF16), flat, triple, VMEM((positions, *pairs), F32),
            VMEM((positions, *pairs), F32), VMEM((positions, *pairs), BF16),
            VMEM((positions, *pairs), BF16), triple, dma((4 + positions // GROUP,)),
        ],
        6 * product + 5 * inner, 4 * size, [HBM, HBM],
    )
    grad_home = exchange(grad_normed.reshape(sent))
    (projected,) = call(
        project_kernel, [shaped(spread, BF16)], [VMEM, ON_CHIP] + [VMEM] * 4,
        [kept, used, w_query, w_key, w_value, w_out],
        [wide] + [part] * 4, 4 * product + 2 * inner, 2 * size,
    )
    projected_home = exchange(projected.reshape(sent))
    grad_hidden, head, tail = call(
        grad_hidden_kernel, [shaped(home, BF16), shaped(edge, BF16), shaped(edge, BF16)],
        [SMEM, SMEM, VMEM, VMEM, ON_CHIP],
        [frame_count, row_count, cotangent, hidden, grad_home], [], 0, 5 * size,
    )
    above, below = share_rows(head, tail)
    (video_grad,) = call(
        video_grad_kernel, [shaped(home, BF16)], [SMEM, SMEM, VMEM, ON_CHIP, ON_CHIP, VMEM],
        [frame_count, row_count, grad_hidden, above, below, w_conv], [VMEM(padded, BF16)],
        9 * product, 3 * size,
    )
    (encoded,) = call(
        encode_kernel, [shaped(home, BF16)], [SMEM, SMEM, ON_CHIP, ON_CHIP],
        [frame_count, row_count, hidden, projected_home],
        [VMEM(home, BF16), dma((frames,))], 0, 3 * size, [HBM],
    )
    return encoded, video_grad


def solution(mesh):
    field = P("tm", "space", None, None)
    in_specs = (field, field) + (P(),) * 7

    return jax.shard_map(
        body, mesh=mesh, in_specs=in_specs, out_specs=(field, field), check_vma=False
    )
```

```python
import jax
import jax.numpy as jnp
from jax import lax
from jax.experimental import pallas as pl
from jax.experimental.pallas import tpu as pltpu
from jax.sharding import PartitionSpec as P


BF16 = jnp.bfloat16
F32 = jnp.float32
GROUP = 4
LANES = 128
VMEM = pltpu.VMEM
SMEM = pltpu.SMEM
HBM = pltpu.HBM
ON_CHIP = object()


def dot(a, b, contract=(1, 0)):
    return lax.dot_general(
        a, b, (((contract[0],), (contract[1],)), ((), ())), preferred_element_type=F32
    )


def specs(*spaces):
    return [pl.BlockSpec(memory_space=space) for space in spaces]


def cost(flops, moved):
    return pl.CostEstimate(flops=flops, bytes_accessed=moved, transcendentals=0)


def edges_kernel(row_count, field, head, tail, sems):
    rows_here = row_count[lax.axis_index("space")]
    first = pltpu.make_async_copy(field.at[:, 0], head, sems.at[0])
    last = pltpu.make_async_copy(field.at[:, rows_here - 1], tail, sems.at[1])
    first.start()
    last.start()
    first.wait()
    last.wait()


def fill_halo(extended, field, above, below, rows_here):
    slots = field.shape[1]
    extended[:, 1 : 1 + slots] = field[...]
    extended[:, 0] = above[...]
    extended[:, 1 + rows_here] = below[...]


def convolve_frame(extended, weight, frame, flipped):
    _, padded, columns, channels = extended.shape
    tokens = (padded - 2) * columns
    column = lax.broadcasted_iota(jnp.int32, (tokens, channels), 0) % columns
    total = None
    for b in range(3):
        part = None
        for a in range(3):
            view = extended[frame, a : a + padded - 2].reshape(tokens, channels)
            if flipped:
                term = dot(view, weight[2 - a, 2 - b], (1, 1))
            else:
                term = dot(view, weight[a, b])
            part = term if part is None else part + term
        if b == 0:
            part = jnp.where(column == 0, 0.0, pltpu.roll(part, 1, 0))
        elif b == 2:
            part = jnp.where(column == columns - 1, 0.0, pltpu.roll(part, tokens - 1, 0))
        total = part if total is None else total + part
    return total


def token_mask(frame, frames_here, rows_here, columns, shape):
    row = lax.broadcasted_iota(jnp.int32, shape, 0) // columns
    return (row < rows_here) & (frame < frames_here)


def inverse_rms(hidden):
    return lax.rsqrt(jnp.mean(hidden * hidden, axis=-1, keepdims=True) + 1e-06)


def hidden_kernel(
    frame_count, row_count, field, above, below, weight, hidden_out, normed_out, extended
):
    frames_here = frame_count[lax.axis_index("tm")]
    rows_here = row_count[lax.axis_index("space")]
    frames, slots, columns, channels = field.shape
    tokens = slots * columns
    fill_halo(extended, field, above, below, rows_here)

    def step(frame, carry):
        total = convolve_frame(extended, weight, frame, False)
        used = token_mask(frame, frames_here, rows_here, columns, total.shape)
        center = field[frame].reshape(tokens, channels).astype(F32)
        hidden = jnp.where(used, center + total, 0.0).astype(BF16)
        hidden_out[:, frame] = hidden.reshape(hidden_out.shape[0], -1, channels)
        hidden_f = hidden.astype(F32)
        normed = (hidden_f * inverse_rms(hidden_f)).astype(BF16)
        normed_out[:, frame] = normed.reshape(normed_out.shape[0], -1, channels)
        return carry

    lax.fori_loop(0, frames, step, 0)


def load_position(spread, position, positions, scale=None):
    parts = []
    for h in range(spread.shape[0]):
        rows = spread[h, pl.ds(position, spread.shape[1] // positions, stride=positions), :]
        parts.append((rows if scale is None else rows * scale).astype(BF16))
    return jnp.concatenate(parts, axis=1)


def store_position(spread, position, positions, rows):
    for h in range(spread.shape[0]):
        part = rows[:, h * LANES : (h + 1) * LANES]
        spread[h, pl.ds(position, rows.shape[0], stride=positions), :] = part


def widen(source, spread):
    for h in range(spread.shape[0]):
        part = source[:, :, h * LANES : (h + 1) * LANES].astype(F32)
        spread[h] = part.reshape(spread.shape[1], LANES)


def narrow(spread, held, target, sems):
    frames, positions, _ = held.shape
    pieces = 4
    size = frames // pieces
    copies = []
    for i in range(pieces):
        here = slice(i * size, (i + 1) * size)
        for h in range(spread.shape[0]):
            part = spread[h, i * size * positions : (i + 1) * size * positions]
            part = part.reshape(size, positions, LANES)
            held[here, :, h * LANES : (h + 1) * LANES] = part.astype(BF16)
        copy = pltpu.make_async_copy(held.at[here], target.at[here], sems.at[i])
        copy.start()
        copies.append(copy)
    for copy in copies:
        copy.wait()


def send_kernel(field, out, held, sems):
    frames = field.shape[0]
    arrive = [
        pltpu.make_async_copy(field.at[f], held.at[f], sems.at[0, f]) for f in range(frames)
    ]
    leave = [
        pltpu.make_async_copy(held.at[f], out.at[:, f], sems.at[1, f]) for f in range(frames)
    ]
    for copy in arrive:
        copy.start()
    for f in range(frames):
        arrive[f].wait()
        leave[f].start()
    for copy in leave:
        copy.wait()


def grads_kernel(
    cotangent, used, w_out, w_query, w_key, w_value, folded, mixed, spread, ordered, attended
):
    all_frames, positions, channels = cotangent.shape
    mixed[...] = (dot(w_query[...], w_key[...], (1, 1)) * channels ** (-0.5)).astype(BF16)
    widen(cotangent, spread)
    for first in range(0, positions, GROUP):
        for p in range(first, first + GROUP):
            here = slice(p * all_frames, (p + 1) * all_frames)
            ordered[here] = load_position(spread, p, positions, used[...])
        here = slice(first * all_frames, (first + GROUP) * all_frames)
        attended[here] = dot(ordered[here], w_out[...], (1, 1)).astype(BF16)
        grads = dot(attended[here], w_value[...], (1, 1)).astype(BF16)
        folded[first : first + GROUP] = grads.reshape(GROUP, all_frames, channels)


def softmax_probs(query, key, allowed, scale):
    scores = jnp.where(allowed, dot(key, query, (1, 1)) * scale, -1e30)
    expo = jnp.exp(scores - jnp.max(scores, axis=0, keepdims=True))
    return expo * (1.0 / jnp.sum(expo, axis=0, keepdims=True))


def allowed_pairs(used):
    tile = (used.shape[0], used.shape[0])
    source = lax.broadcasted_iota(jnp.int32, tile, 0)
    reader = lax.broadcasted_iota(jnp.int32, tile, 1)
    return (source <= reader) & (used[...] > 0.0)


def attention_kernel(
    normed, folded, used, mixed, grad_normed, kept,
    weights, bias, spread, result, out, ordered, sides, products, mix, inner, direct, sems,
):
    all_frames, positions, channels = normed.shape
    pieces = positions // GROUP
    loads = [
        pltpu.make_async_copy(mixed, weights, sems.at[0]),
        pltpu.make_async_copy(folded, sides.at[:, all_frames:], sems.at[1]),
    ]
    for copy in loads:
        copy.start()
    widen(normed, spread)
    bias[...] = jnp.where(allowed_pairs(used), 0.0, -1e30)
    keeps = []

    def rows_of(p):
        return slice(p * all_frames, (p + 1) * all_frames)

    def group_of(first):
        return slice(first * all_frames, (first + GROUP) * all_frames)

    def project_group(first):
        group = group_of(first)
        for p in range(first, first + GROUP):
            ordered[rows_of(p)] = load_position(spread, p, positions)
        keep = pltpu.make_async_copy(
            ordered.at[group], kept.at[group], sems.at[pieces + first // GROUP]
        )
        keep.start()
        keeps.append(keep)
        queries = dot(ordered[group], weights[...]).astype(BF16)
        sides[first : first + GROUP, :all_frames] = queries.reshape(GROUP, all_frames, channels)

    def pair_products(p):
        products[p] = dot(ordered[rows_of(p)], sides[p], (1, 1))

    def softmax(p):
        logits = products[p, :, :all_frames] + bias[...]
        expo = jnp.exp(logits - jnp.max(logits, axis=0, keepdims=True))
        probs = expo * (1.0 / jnp.sum(expo, axis=0, keepdims=True))
        low = probs.astype(BF16)
        grad = products[p, :, all_frames:]
        delta = jnp.sum(low.astype(F32) * grad, axis=0, keepdims=True)
        mix[p, :, :all_frames] = (probs * (grad - delta)).astype(BF16)
        mix[p, :, all_frames:] = low

    def back_products(p):
        here = rows_of(p)
        direct[here] = dot(mix[p], sides[p])
        inner[here] = dot(mix[p, :, :all_frames], ordered[here], (0, 0)).astype(BF16)

    def back_group(first):
        group = group_of(first)
        total = dot(inner[group], weights[...], (1, 1)) + direct[group]
        total = total.astype(BF16).astype(F32)
        for j in range(GROUP):
            part = total[j * all_frames : (j + 1) * all_frames]
            store_position(result, first + j, positions, part)

    loads[0].wait()
    project_group(0)
    loads[1].wait()
    for first in range(0, positions, GROUP):
        group = range(first, first + GROUP)
        for p in group:
            pair_products(p)
        if first + GROUP < positions:
            project_group(first + GROUP)
        for p in group:
            softmax(p)
        if first > 0:
            back_group(first - GROUP)
        for p in group:
            back_products(p)
    back_group(positions - GROUP)
    narrow(result, out, grad_normed, sems)
    for copy in keeps:
        copy.wait()


def project_kernel(
    ordered, used, w_query, w_key, w_value, w_out, projected,
    spread, query_s, key_s, value_s, attended,
):
    all_frames, positions, channels = projected.shape
    allowed = allowed_pairs(used)
    scale = channels ** (-0.5)

    def step(i, carry):
        first = pl.multiple_of(i * GROUP * all_frames, GROUP * all_frames)
        rows = ordered[pl.ds(first, GROUP * all_frames)]
        query_s[...] = dot(rows, w_query[...]).astype(BF16)
        key_s[...] = dot(rows, w_key[...]).astype(BF16)
        value_s[...] = dot(rows, w_value[...]).astype(BF16)
        for j in range(GROUP):
            here = slice(j * all_frames, (j + 1) * all_frames)
            low = softmax_probs(query_s[here], key_s[here], allowed, scale).astype(BF16)
            attended[here] = dot(low, value_s[here], (0, 0)).astype(BF16)
        total = dot(attended[...], w_out[...]).astype(BF16).astype(F32)
        for j in range(GROUP):
            part = total[j * all_frames : (j + 1) * all_frames]
            store_position(spread, i * GROUP + j, positions, part)
        return carry

    lax.fori_loop(0, positions // GROUP, step, 0)
    for h in range(spread.shape[0]):
        part = spread[h].reshape(all_frames, positions, LANES)
        projected[:, :, h * LANES : (h + 1) * LANES] = part.astype(BF16)


def encode_kernel(frame_count, row_count, hidden, projected, encoded, held, sems):
    frames_here = frame_count[lax.axis_index("tm")]
    rows_here = row_count[lax.axis_index("space")]
    frames, slots, columns, channels = encoded.shape
    tokens = slots * columns
    copies = []
    for frame in range(frames):
        total = hidden[:, frame].astype(F32) + projected[:, frame].astype(F32)
        total = total.reshape(tokens, channels)
        used = token_mask(frame, frames_here, rows_here, columns, total.shape)
        total = jnp.where(used, total, 0.0).astype(BF16)
        held[frame] = total.reshape(slots, columns, channels)
        copy = pltpu.make_async_copy(held.at[frame], encoded.at[frame], sems.at[frame])
        copy.start()
        copies.append(copy)
    for copy in copies:
        copy.wait()


def grad_hidden_kernel(
    frame_count, row_count, cotangent, hidden, grad_normed, grad_hidden, head, tail
):
    frames_here = frame_count[lax.axis_index("tm")]
    rows_here = row_count[lax.axis_index("space")]
    frames, slots, columns, channels = cotangent.shape
    tokens = slots * columns

    def step(frame, carry):
        hid = hidden[:, frame].astype(F32).reshape(tokens, channels)
        grad = grad_normed[:, frame].astype(F32).reshape(tokens, channels)
        outer = cotangent[frame].astype(F32).reshape(tokens, channels)
        inv = inverse_rms(hid)
        inner = jnp.mean(grad * hid, axis=-1, keepdims=True)
        total = outer + inv * grad - (inv * inv * inv * inner) * hid
        used = token_mask(frame, frames_here, rows_here, columns, total.shape)
        total = jnp.where(used, total, 0.0).astype(BF16)
        grad_hidden[frame] = total.reshape(slots, columns, channels)
        return carry

    lax.fori_loop(0, frames, step, 0)
    head[...] = grad_hidden[:, 0]
    tail[...] = grad_hidden[:, rows_here - 1]


def video_grad_kernel(frame_count, row_count, field, above, below, weight, out, extended):
    frames_here = frame_count[lax.axis_index("tm")]
    rows_here = row_count[lax.axis_index("space")]
    frames, slots, columns, channels = field.shape
    tokens = slots * columns
    fill_halo(extended, field, above, below, rows_here)

    def step(frame, carry):
        total = convolve_frame(extended, weight, frame, True)
        used = token_mask(frame, frames_here, rows_here, columns, total.shape)
        center = field[frame].reshape(tokens, channels).astype(F32)
        total = jnp.where(used, center + total, 0.0).astype(BF16)
        out[frame] = total.reshape(slots, columns, channels)
        return carry

    lax.fori_loop(0, frames, step, 0)


def share_rows(head, tail):
    ends = lax.axis_size("space") - 1
    above = lax.ppermute(tail, "space", [(i, i + 1) for i in range(ends)])
    below = lax.ppermute(head, "space", [(i + 1, i) for i in range(ends)])
    return above, below


def exchange(blocks):
    return lax.all_to_all(blocks, "tm", split_axis=0, concat_axis=0, tiled=True)


def body(video, cotangent, frame_count, row_count, w_conv, w_query, w_key, w_value, w_out):
    frames, slots, columns, channels = video.shape
    blocks = lax.axis_size("tm")
    positions = slots * columns // blocks
    all_frames = frames * blocks
    shaped = jax.ShapeDtypeStruct
    home = (frames, slots, columns, channels)
    sent = (blocks, frames, positions, channels)
    spread = (all_frames, positions, channels)
    ordered = (positions, all_frames, channels)
    edge = (frames, columns, channels)
    padded = (frames, slots + 2, columns, channels)
    size = 2 * frames * slots * columns * channels
    product = 2 * frames * slots * columns * channels * channels
    inner = 2 * positions * all_frames * all_frames * channels

    def call(kernel, outs, ins, args, scratch, flops, moved, out_spaces=None):
        args = [
            pltpu.with_memory_space_constraint(x, VMEM) if space is ON_CHIP else x
            for x, space in zip(args, ins)
        ]
        ins = [VMEM if space is ON_CHIP else space for space in ins]
        return pl.pallas_call(
            kernel,
            out_shape=outs,
            in_specs=specs(*ins),
            out_specs=specs(*(out_spaces or [VMEM] * len(outs))),
            scratch_shapes=scratch,
            cost_estimate=cost(flops, moved),
        )(*args)

    dma = pltpu.SemaphoreType.DMA
    wide = VMEM((channels // LANES, all_frames * positions, LANES), F32)
    flat = VMEM((all_frames * positions, channels), BF16)
    part = VMEM((GROUP * all_frames, channels), BF16)
    chunked = (frames, blocks, positions, channels)

    (outgoing,) = call(
        send_kernel, [shaped(sent, BF16)], [HBM], [cotangent.reshape(chunked)],
        [VMEM(chunked, BF16), dma((2, frames))], 0, size, [HBM],
    )
    grads_in = exchange(outgoing).reshape(spread)
    head, tail = call(
        edges_kernel, [VMEM(edge, BF16)] * 2, [SMEM, HBM], [row_count, video],
        [dma((2,))], 0, size // 4,
    )
    above, below = share_rows(head, tail)
    hidden, normed = call(
        hidden_kernel, [shaped(sent, BF16)] * 2, [SMEM, SMEM, VMEM, ON_CHIP, ON_CHIP, VMEM],
        [frame_count, row_count, video, above, below, w_conv], [VMEM(padded, BF16)],
        9 * product, 4 * size,
    )
    normed_in = exchange(normed).reshape(spread)
    slot = lax.broadcasted_iota(jnp.int32, (blocks, frames, LANES), 1)
    used = (slot < frame_count[:, None, None]).astype(F32).reshape(all_frames, LANES)
    folded, mixed = call(
        grads_kernel, [shaped(ordered, BF16), shaped((channels, channels), BF16)],
        [ON_CHIP, ON_CHIP] + [VMEM] * 4, [grads_in, used, w_out, w_query, w_key, w_value],
        [wide, flat, flat], 2 * product, 2 * size,
    )
    pairs = (all_frames, all_frames)
    double = (positions, 2 * all_frames, channels)
    grad_normed, kept = call(
        attention_kernel,
        [shaped(spread, BF16), shaped((all_frames * positions, channels), BF16)],
        [ON_CHIP, HBM, ON_CHIP, HBM], [normed_in, folded, used, mixed],
        [
            VMEM((channels, channels), BF16), VMEM(pairs, F32), wide, wide, VMEM(spread, BF16),
            flat, VMEM(double, BF16), VMEM((positions, all_frames, 2 * all_frames), F32),
            VMEM((positions, all_frames, 2 * all_frames), BF16), flat,
            VMEM((all_frames * positions, channels), F32), dma((2 * positions // GROUP,)),
        ],
        2 * product + 5 * inner, 4 * size, [HBM, HBM],
    )
    grad_home = exchange(grad_normed.reshape(sent))
    (projected,) = call(
        project_kernel, [shaped(spread, BF16)], [VMEM, ON_CHIP] + [VMEM] * 4,
        [kept, used, w_query, w_key, w_value, w_out],
        [wide] + [part] * 4, 4 * product + 2 * inner, 2 * size,
    )
    projected_home = exchange(projected.reshape(sent))
    grad_hidden, head, tail = call(
        grad_hidden_kernel, [shaped(home, BF16), shaped(edge, BF16), shaped(edge, BF16)],
        [SMEM, SMEM, VMEM, VMEM, ON_CHIP],
        [frame_count, row_count, cotangent, hidden, grad_home], [], 0, 5 * size,
    )
    above, below = share_rows(head, tail)
    (video_grad,) = call(
        video_grad_kernel, [shaped(home, BF16)], [SMEM, SMEM, VMEM, ON_CHIP, ON_CHIP, VMEM],
        [frame_count, row_count, grad_hidden, above, below, w_conv], [VMEM(padded, BF16)],
        9 * product, 3 * size,
    )
    (encoded,) = call(
        encode_kernel, [shaped(home, BF16)], [SMEM, SMEM, ON_CHIP, ON_CHIP],
        [frame_count, row_count, hidden, projected_home],
        [VMEM(home, BF16), dma((frames,))], 0, 3 * size, [HBM],
    )
    return encoded, video_grad


def solution(mesh):
    field = P("tm", "space", None, None)
    in_specs = (field, field) + (P(),) * 7

    return jax.shard_map(
        body, mesh=mesh, in_specs=in_specs, out_specs=(field, field), check_vma=False
    )
```

```python
import jax
import jax.numpy as jnp
from jax import lax
from jax.experimental import pallas as pl
from jax.experimental.pallas import tpu as pltpu
from jax.sharding import PartitionSpec as P


BF16 = jnp.bfloat16
F32 = jnp.float32
GROUP = 4
LANES = 128
RING = 4
VMEM = pltpu.VMEM
SMEM = pltpu.SMEM
HBM = pltpu.HBM
ON_CHIP = object()


def dot(a, b, contract=(1, 0)):
    return lax.dot_general(
        a, b, (((contract[0],), (contract[1],)), ((), ())), preferred_element_type=F32
    )


def specs(*spaces):
    return [pl.BlockSpec(memory_space=space) for space in spaces]


def cost(flops, moved):
    return pl.CostEstimate(flops=flops, bytes_accessed=moved, transcendentals=0)


def fill_halo(extended, field, above, below, rows_here):
    slots = field.shape[1]
    extended[:, 1 : 1 + slots] = field[...]
    extended[:, 0] = above[...]
    extended[:, 1 + rows_here] = below[...]


def convolve_frame(extended, weight, frame, flipped):
    _, padded, columns, channels = extended.shape
    tokens = (padded - 2) * columns
    column = lax.broadcasted_iota(jnp.int32, (tokens, channels), 0) % columns
    total = None
    for b in range(3):
        part = None
        for a in range(3):
            view = extended[frame, a : a + padded - 2].reshape(tokens, channels)
            if flipped:
                term = dot(view, weight[2 - a, 2 - b], (1, 1))
            else:
                term = dot(view, weight[a, b])
            part = term if part is None else part + term
        if b == 0:
            part = jnp.where(column == 0, 0.0, pltpu.roll(part, 1, 0))
        elif b == 2:
            part = jnp.where(column == columns - 1, 0.0, pltpu.roll(part, tokens - 1, 0))
        total = part if total is None else total + part
    return total


def token_mask(frame, frames_here, rows_here, columns, shape):
    row = lax.broadcasted_iota(jnp.int32, shape, 0) // columns
    return (row < rows_here) & (frame < frames_here)


def inverse_rms(hidden):
    return lax.rsqrt(jnp.mean(hidden * hidden, axis=-1, keepdims=True) + 1e-06)


def hidden_kernel(
    frame_count, row_count, field, above, below, weight, hidden_out, normed_out, extended
):
    frames_here = frame_count[lax.axis_index("tm")]
    rows_here = row_count[lax.axis_index("space")]
    frames, slots, columns, channels = field.shape
    tokens = slots * columns
    fill_halo(extended, field, above, below, rows_here)

    def step(frame, carry):
        total = convolve_frame(extended, weight, frame, False)
        used = token_mask(frame, frames_here, rows_here, columns, total.shape)
        center = field[frame].reshape(tokens, channels).astype(F32)
        hidden = jnp.where(used, center + total, 0.0).astype(BF16)
        hidden_out[:, frame] = hidden.reshape(hidden_out.shape[0], -1, channels)
        hidden_f = hidden.astype(F32)
        normed = (hidden_f * inverse_rms(hidden_f)).astype(BF16)
        normed_out[:, frame] = normed.reshape(normed_out.shape[0], -1, channels)
        return carry

    lax.fori_loop(0, frames, step, 0)


def load_position(spread, position, positions, scale=None):
    parts = []
    for h in range(spread.shape[0]):
        rows = spread[h, pl.ds(position, spread.shape[1] // positions, stride=positions), :]
        parts.append((rows if scale is None else rows * scale).astype(BF16))
    return jnp.concatenate(parts, axis=1)


def store_position(spread, position, positions, rows):
    for h in range(spread.shape[0]):
        part = rows[:, h * LANES : (h + 1) * LANES]
        spread[h, pl.ds(position, rows.shape[0], stride=positions), :] = part


def widen(source, spread):
    for h in range(spread.shape[0]):
        part = source[:, :, h * LANES : (h + 1) * LANES].astype(F32)
        spread[h] = part.reshape(spread.shape[1], LANES)


def narrow(spread, held, target, sems):
    frames, positions, _ = held.shape
    pieces = 4
    size = frames // pieces
    copies = []
    for i in range(pieces):
        here = slice(i * size, (i + 1) * size)
        for h in range(spread.shape[0]):
            part = spread[h, i * size * positions : (i + 1) * size * positions]
            part = part.reshape(size, positions, LANES)
            held[here, :, h * LANES : (h + 1) * LANES] = part.astype(BF16)
        copy = pltpu.make_async_copy(held.at[here], target.at[here], sems.at[i])
        copy.start()
        copies.append(copy)
    for copy in copies:
        copy.wait()


def split_kernel(row_count, video, field, head, tail, *rest):
    *outs, held, sems, edge_sems = rest
    rows_here = row_count[lax.axis_index("space")]
    first = pltpu.make_async_copy(video.at[:, 0], head, edge_sems.at[0])
    last = pltpu.make_async_copy(video.at[:, rows_here - 1], tail, edge_sems.at[1])
    frames = field.shape[0]
    rings = len(outs)
    level = lax.axis_index("tm") // RING
    arrive = [
        pltpu.make_async_copy(field.at[f], held.at[f], sems.at[rings, f]) for f in range(frames)
    ]
    for copy in arrive:
        copy.start()
    first.start()
    last.start()
    leave = []
    for f in range(frames):
        arrive[f].wait()
        for k in range(rings):
            start = (level + k) % rings * RING
            copy = pltpu.make_async_copy(
                held.at[f, pl.ds(start, RING)], outs[k].at[:, f], sems.at[k, f]
            )
            copy.start()
            leave.append(copy)
    for copy in leave + [first, last]:
        copy.wait()


def turn_kernel(*refs):
    *refs, held, sems = refs
    rings = held.shape[0]
    blocks, outs = refs[:rings], refs[rings:]
    place = lax.axis_index("tm") % RING
    arrive = [pltpu.make_async_copy(blocks[k], held.at[k], sems.at[k]) for k in range(rings)]
    for copy in arrive:
        copy.start()
    for copy in arrive:
        copy.wait()
    leave = [
        pltpu.make_async_copy(held.at[:, (place + j) % RING], outs[j], sems.at[rings + j])
        for j in range(RING)
    ]
    for copy in leave:
        copy.start()
    for copy in leave:
        copy.wait()


def grads_kernel(
    a, b, c, d, used, w_out, w_query, w_key, w_value, folded, mixed,
    cotangent, spread, ordered, attended, sems,
):
    all_frames, positions, channels = cotangent.shape
    rings, frames = a.shape[:2]
    here = lax.axis_index("tm")
    level, place = here // RING, here % RING
    arrive = []
    for j, source in enumerate((a, b, c, d)):
        for k in range(rings):
            block = (level + rings - k) % rings * RING + (place + RING - j) % RING
            target = cotangent.at[pl.ds(block * frames, frames)]
            arrive.append(pltpu.make_async_copy(source.at[k], target, sems.at[j, k]))
    for copy in arrive:
        copy.start()
    mixed[...] = (dot(w_query[...], w_key[...], (1, 1)) * channels ** (-0.5)).astype(BF16)
    for copy in arrive:
        copy.wait()
    widen(cotangent, spread)
    for first in range(0, positions, GROUP):
        for p in range(first, first + GROUP):
            here = slice(p * all_frames, (p + 1) * all_frames)
            ordered[here] = load_position(spread, p, positions, used[...])
        here = slice(first * all_frames, (first + GROUP) * all_frames)
        attended[here] = dot(ordered[here], w_out[...], (1, 1)).astype(BF16)
        grads = dot(attended[here], w_value[...], (1, 1)).astype(BF16)
        folded[first : first + GROUP] = grads.reshape(GROUP, all_frames, channels)


def softmax_probs(query, key, allowed, scale):
    scores = jnp.where(allowed, dot(key, query, (1, 1)) * scale, -1e30)
    expo = jnp.exp(scores - jnp.max(scores, axis=0, keepdims=True))
    return expo * (1.0 / jnp.sum(expo, axis=0, keepdims=True))


def allowed_pairs(used):
    tile = (used.shape[0], used.shape[0])
    source = lax.broadcasted_iota(jnp.int32, tile, 0)
    reader = lax.broadcasted_iota(jnp.int32, tile, 1)
    return (source <= reader) & (used[...] > 0.0)


def attention_kernel(
    normed, folded, used, mixed, grad_normed, kept,
    weights, bias, spread, result, out, ordered, sides, products, mix, inner, direct, sems,
):
    all_frames, positions, channels = normed.shape
    pieces = positions // GROUP
    loads = [
        pltpu.make_async_copy(mixed, weights, sems.at[0]),
        pltpu.make_async_copy(folded, sides.at[:, all_frames:], sems.at[1]),
    ]
    for copy in loads:
        copy.start()
    widen(normed, spread)
    bias[...] = jnp.where(allowed_pairs(used), 0.0, -1e30)
    keeps = []

    def rows_of(p):
        return slice(p * all_frames, (p + 1) * all_frames)

    def group_of(first):
        return slice(first * all_frames, (first + GROUP) * all_frames)

    def project_group(first):
        group = group_of(first)
        for p in range(first, first + GROUP):
            ordered[rows_of(p)] = load_position(spread, p, positions)
        keep = pltpu.make_async_copy(
            ordered.at[group], kept.at[group], sems.at[pieces + first // GROUP]
        )
        keep.start()
        keeps.append(keep)
        queries = dot(ordered[group], weights[...]).astype(BF16)
        sides[first : first + GROUP, :all_frames] = queries.reshape(GROUP, all_frames, channels)

    def pair_products(p):
        products[p] = dot(ordered[rows_of(p)], sides[p], (1, 1))

    def softmax(p):
        logits = products[p, :, :all_frames] + bias[...]
        expo = jnp.exp(logits - jnp.max(logits, axis=0, keepdims=True))
        probs = expo * (1.0 / jnp.sum(expo, axis=0, keepdims=True))
        low = probs.astype(BF16)
        grad = products[p, :, all_frames:]
        delta = jnp.sum(low.astype(F32) * grad, axis=0, keepdims=True)
        mix[p, :, :all_frames] = (probs * (grad - delta)).astype(BF16)
        mix[p, :, all_frames:] = low

    def back_products(p):
        here = rows_of(p)
        direct[here] = dot(mix[p], sides[p])
        inner[here] = dot(mix[p, :, :all_frames], ordered[here], (0, 0)).astype(BF16)

    def back_group(first):
        group = group_of(first)
        total = dot(inner[group], weights[...], (1, 1)) + direct[group]
        total = total.astype(BF16).astype(F32)
        for j in range(GROUP):
            part = total[j * all_frames : (j + 1) * all_frames]
            store_position(result, first + j, positions, part)

    loads[0].wait()
    project_group(0)
    loads[1].wait()
    for first in range(0, positions, GROUP):
        group = range(first, first + GROUP)
        for p in group:
            pair_products(p)
        if first + GROUP < positions:
            project_group(first + GROUP)
        for p in group:
            softmax(p)
        if first > 0:
            back_group(first - GROUP)
        for p in group:
            back_products(p)
    back_group(positions - GROUP)
    narrow(result, out, grad_normed, sems)
    for copy in keeps:
        copy.wait()


def project_kernel(
    ordered, used, w_query, w_key, w_value, w_out, projected,
    spread, query_s, key_s, value_s, attended,
):
    all_frames, positions, channels = projected.shape
    allowed = allowed_pairs(used)
    scale = channels ** (-0.5)

    def step(i, carry):
        first = pl.multiple_of(i * GROUP * all_frames, GROUP * all_frames)
        rows = ordered[pl.ds(first, GROUP * all_frames)]
        query_s[...] = dot(rows, w_query[...]).astype(BF16)
        key_s[...] = dot(rows, w_key[...]).astype(BF16)
        value_s[...] = dot(rows, w_value[...]).astype(BF16)
        for j in range(GROUP):
            here = slice(j * all_frames, (j + 1) * all_frames)
            low = softmax_probs(query_s[here], key_s[here], allowed, scale).astype(BF16)
            attended[here] = dot(low, value_s[here], (0, 0)).astype(BF16)
        total = dot(attended[...], w_out[...]).astype(BF16).astype(F32)
        for j in range(GROUP):
            part = total[j * all_frames : (j + 1) * all_frames]
            store_position(spread, i * GROUP + j, positions, part)
        return carry

    lax.fori_loop(0, positions // GROUP, step, 0)
    for h in range(spread.shape[0]):
        part = spread[h].reshape(all_frames, positions, LANES)
        projected[:, :, h * LANES : (h + 1) * LANES] = part.astype(BF16)


def encode_kernel(frame_count, row_count, hidden, projected, encoded, held, sems):
    frames_here = frame_count[lax.axis_index("tm")]
    rows_here = row_count[lax.axis_index("space")]
    frames, slots, columns, channels = encoded.shape
    tokens = slots * columns
    copies = []
    for frame in range(frames):
        total = hidden[:, frame].astype(F32) + projected[:, frame].astype(F32)
        total = total.reshape(tokens, channels)
        used = token_mask(frame, frames_here, rows_here, columns, total.shape)
        total = jnp.where(used, total, 0.0).astype(BF16)
        held[frame] = total.reshape(slots, columns, channels)
        copy = pltpu.make_async_copy(held.at[frame], encoded.at[frame], sems.at[frame])
        copy.start()
        copies.append(copy)
    for copy in copies:
        copy.wait()


def grad_hidden_kernel(
    frame_count, row_count, cotangent, hidden, grad_normed, grad_hidden, head, tail
):
    frames_here = frame_count[lax.axis_index("tm")]
    rows_here = row_count[lax.axis_index("space")]
    frames, slots, columns, channels = cotangent.shape
    tokens = slots * columns

    def step(frame, carry):
        hid = hidden[:, frame].astype(F32).reshape(tokens, channels)
        grad = grad_normed[:, frame].astype(F32).reshape(tokens, channels)
        outer = cotangent[frame].astype(F32).reshape(tokens, channels)
        inv = inverse_rms(hid)
        inner = jnp.mean(grad * hid, axis=-1, keepdims=True)
        total = outer + inv * grad - (inv * inv * inv * inner) * hid
        used = token_mask(frame, frames_here, rows_here, columns, total.shape)
        total = jnp.where(used, total, 0.0).astype(BF16)
        grad_hidden[frame] = total.reshape(slots, columns, channels)
        return carry

    lax.fori_loop(0, frames, step, 0)
    head[...] = grad_hidden[:, 0]
    tail[...] = grad_hidden[:, rows_here - 1]


def video_grad_kernel(frame_count, row_count, field, above, below, weight, out, extended):
    frames_here = frame_count[lax.axis_index("tm")]
    rows_here = row_count[lax.axis_index("space")]
    frames, slots, columns, channels = field.shape
    tokens = slots * columns
    fill_halo(extended, field, above, below, rows_here)

    def step(frame, carry):
        total = convolve_frame(extended, weight, frame, True)
        used = token_mask(frame, frames_here, rows_here, columns, total.shape)
        center = field[frame].reshape(tokens, channels).astype(F32)
        total = jnp.where(used, center + total, 0.0).astype(BF16)
        out[frame] = total.reshape(slots, columns, channels)
        return carry

    lax.fori_loop(0, frames, step, 0)


def share_rows(head, tail):
    ends = lax.axis_size("space") - 1
    above = lax.ppermute(tail, "space", [(i, i + 1) for i in range(ends)])
    below = lax.ppermute(head, "space", [(i + 1, i) for i in range(ends)])
    return above, below


def exchange(blocks):
    return lax.all_to_all(blocks, "tm", split_axis=0, concat_axis=0, tiled=True)


def body(video, cotangent, frame_count, row_count, w_conv, w_query, w_key, w_value, w_out):
    frames, slots, columns, channels = video.shape
    blocks = lax.axis_size("tm")
    positions = slots * columns // blocks
    all_frames = frames * blocks
    shaped = jax.ShapeDtypeStruct
    home = (frames, slots, columns, channels)
    sent = (blocks, frames, positions, channels)
    spread = (all_frames, positions, channels)
    ordered = (positions, all_frames, channels)
    edge = (frames, columns, channels)
    padded = (frames, slots + 2, columns, channels)
    size = 2 * frames * slots * columns * channels
    product = 2 * frames * slots * columns * channels * channels
    inner = 2 * positions * all_frames * all_frames * channels

    def call(kernel, outs, ins, args, scratch, flops, moved, out_spaces=None):
        args = [
            pltpu.with_memory_space_constraint(x, VMEM) if space is ON_CHIP else x
            for x, space in zip(args, ins)
        ]
        ins = [VMEM if space is ON_CHIP else space for space in ins]
        return pl.pallas_call(
            kernel,
            out_shape=outs,
            in_specs=specs(*ins),
            out_specs=specs(*(out_spaces or [VMEM] * len(outs))),
            scratch_shapes=scratch,
            cost_estimate=cost(flops, moved),
        )(*args)

    dma = pltpu.SemaphoreType.DMA
    wide = VMEM((channels // LANES, all_frames * positions, LANES), F32)
    flat = VMEM((all_frames * positions, channels), BF16)
    part = VMEM((GROUP * all_frames, channels), BF16)
    chunked = (frames, blocks, positions, channels)

    rings = blocks // RING
    parcel = (RING, frames, positions, channels)
    bundle = (rings, frames, positions, channels)
    head, tail, *parcels = call(
        split_kernel, [VMEM(edge, BF16)] * 2 + [shaped(parcel, BF16)] * rings, [SMEM, HBM, HBM],
        [row_count, video, cotangent.reshape(chunked)],
        [VMEM(chunked, BF16), dma((rings + 1, frames)), dma((2,))], 0, size,
        [VMEM] * 2 + [HBM] * rings,
    )
    above, below = share_rows(head, tail)
    for k in range(1, rings):
        parcels[k] = lax.ppermute(
            parcels[k], "tm", [(i, (i + k * RING) % blocks) for i in range(blocks)]
        )
    hidden, normed = call(
        hidden_kernel, [shaped(sent, BF16)] * 2, [SMEM, SMEM, ON_CHIP, ON_CHIP, ON_CHIP, ON_CHIP],
        [frame_count, row_count, video, above, below, w_conv], [VMEM(padded, BF16)],
        9 * product, 4 * size,
    )
    normed_in = exchange(normed).reshape(spread)
    slot = lax.broadcasted_iota(jnp.int32, (blocks, frames, LANES), 1)
    used = (slot < frame_count[:, None, None]).astype(F32).reshape(all_frames, LANES)
    bundles = list(call(
        turn_kernel, [shaped(bundle, BF16)] * RING, [HBM] * rings, parcels,
        [VMEM((rings, *parcel), BF16), dma((rings + RING,))], 0, size, [HBM] * RING,
    ))
    for j in range(1, RING):
        ring = [(i, i // RING * RING + (i + j) % RING) for i in range(blocks)]
        bundles[j] = lax.ppermute(bundles[j], "tm", ring)
    folded, mixed = call(
        grads_kernel, [shaped(ordered, BF16), shaped((channels, channels), BF16)],
        [HBM] * RING + [ON_CHIP] + [VMEM] * 4,
        [*bundles, used, w_out, w_query, w_key, w_value],
        [VMEM(spread, BF16), wide, flat, flat, dma((RING, rings))], 2 * product, 2 * size,
    )
    pairs = (all_frames, all_frames)
    double = (positions, 2 * all_frames, channels)
    grad_normed, kept = call(
        attention_kernel,
        [shaped(spread, BF16), shaped((all_frames * positions, channels), BF16)],
        [ON_CHIP, HBM, ON_CHIP, HBM], [normed_in, folded, used, mixed],
        [
            VMEM((channels, channels), BF16), VMEM(pairs, F32), wide, wide, VMEM(spread, BF16),
            flat, VMEM(double, BF16), VMEM((positions, all_frames, 2 * all_frames), F32),
            VMEM((positions, all_frames, 2 * all_frames), BF16), flat,
            VMEM((all_frames * positions, channels), F32), dma((2 * positions // GROUP,)),
        ],
        2 * product + 5 * inner, 4 * size, [HBM, HBM],
    )
    grad_home = exchange(grad_normed.reshape(sent))
    (projected,) = call(
        project_kernel, [shaped(spread, BF16)], [VMEM, ON_CHIP] + [VMEM] * 4,
        [kept, used, w_query, w_key, w_value, w_out],
        [wide] + [part] * 4, 4 * product + 2 * inner, 2 * size,
    )
    projected_home = exchange(projected.reshape(sent))
    grad_hidden, head, tail = call(
        grad_hidden_kernel, [shaped(home, BF16), shaped(edge, BF16), shaped(edge, BF16)],
        [SMEM, SMEM, VMEM, VMEM, ON_CHIP],
        [frame_count, row_count, cotangent, hidden, grad_home], [], 0, 5 * size,
    )
    above, below = share_rows(head, tail)
    (video_grad,) = call(
        video_grad_kernel, [shaped(home, BF16)], [SMEM, SMEM, VMEM, ON_CHIP, ON_CHIP, VMEM],
        [frame_count, row_count, grad_hidden, above, below, w_conv], [VMEM(padded, BF16)],
        9 * product, 3 * size,
    )
    (encoded,) = call(
        encode_kernel, [shaped(home, BF16)], [SMEM, SMEM, ON_CHIP, ON_CHIP],
        [frame_count, row_count, hidden, projected_home],
        [VMEM(home, BF16), dma((frames,))], 0, 3 * size, [HBM],
    )
    return encoded, video_grad


def solution(mesh):
    field = P("tm", "space", None, None)
    in_specs = (field, field) + (P(),) * 7

    return jax.shard_map(
        body, mesh=mesh, in_specs=in_specs, out_specs=(field, field), check_vma=False
    )
```

```python
import jax
import jax.numpy as jnp
from jax import lax
from jax.experimental import pallas as pl
from jax.experimental.pallas import tpu as pltpu
from jax.sharding import PartitionSpec as P


BF16 = jnp.bfloat16
F32 = jnp.float32
GROUP = 4
LANES = 128
TILE = 16
VMEM = pltpu.VMEM
SMEM = pltpu.SMEM
HBM = pltpu.HBM
ON_CHIP = object()


def dot(a, b, contract=(1, 0)):
    return lax.dot_general(
        a, b, (((contract[0],), (contract[1],)), ((), ())), preferred_element_type=F32
    )


def specs(*spaces):
    return [pl.BlockSpec(memory_space=space) for space in spaces]


def cost(flops, moved):
    return pl.CostEstimate(flops=flops, bytes_accessed=moved, transcendentals=0)


def edges_kernel(row_count, field, head, tail, sems):
    rows_here = row_count[lax.axis_index("space")]
    first = pltpu.make_async_copy(field.at[:, 0], head, sems.at[0])
    last = pltpu.make_async_copy(field.at[:, rows_here - 1], tail, sems.at[1])
    first.start()
    last.start()
    first.wait()
    last.wait()


def fill_halo(extended, field, above, below, rows_here):
    slots = field.shape[1]
    extended[:, 1 : 1 + slots] = field[...]
    extended[:, 0] = above[...]
    extended[:, 1 + rows_here] = below[...]


def convolve_frame(extended, weight, frame, flipped):
    _, padded, columns, channels = extended.shape
    tokens = (padded - 2) * columns
    column = lax.broadcasted_iota(jnp.int32, (tokens, channels), 0) % columns
    total = None
    for b in range(3):
        part = None
        for a in range(3):
            view = extended[frame, a : a + padded - 2].reshape(tokens, channels)
            if flipped:
                term = dot(view, weight[2 - a, 2 - b], (1, 1))
            else:
                term = dot(view, weight[a, b])
            part = term if part is None else part + term
        if b == 0:
            part = jnp.where(column == 0, 0.0, pltpu.roll(part, 1, 0))
        elif b == 2:
            part = jnp.where(column == columns - 1, 0.0, pltpu.roll(part, tokens - 1, 0))
        total = part if total is None else total + part
    return total


def token_mask(frame, frames_here, rows_here, columns, shape):
    row = lax.broadcasted_iota(jnp.int32, shape, 0) // columns
    return (row < rows_here) & (frame < frames_here)


def inverse_rms(hidden):
    return lax.rsqrt(jnp.mean(hidden * hidden, axis=-1, keepdims=True) + 1e-06)


def hidden_kernel(
    frame_count, row_count, field, above, below, weight, hidden_out, normed_out, extended
):
    frames_here = frame_count[lax.axis_index("tm")]
    rows_here = row_count[lax.axis_index("space")]
    frames, slots, columns, channels = field.shape
    tokens = slots * columns
    fill_halo(extended, field, above, below, rows_here)

    def step(frame, carry):
        total = convolve_frame(extended, weight, frame, False)
        used = token_mask(frame, frames_here, rows_here, columns, total.shape)
        center = field[frame].reshape(tokens, channels).astype(F32)
        hidden = jnp.where(used, center + total, 0.0).astype(BF16)
        hidden_out[:, frame] = hidden.reshape(hidden_out.shape[0], -1, channels)
        hidden_f = hidden.astype(F32)
        normed = (hidden_f * inverse_rms(hidden_f)).astype(BF16)
        normed_out[:, frame] = normed.reshape(normed_out.shape[0], -1, channels)
        return carry

    lax.fori_loop(0, frames, step, 0)


def load_position(spread, position, positions, scale=None):
    parts = []
    for h in range(spread.shape[0]):
        rows = spread[h, pl.ds(position, spread.shape[1] // positions, stride=positions), :]
        parts.append((rows if scale is None else rows * scale).astype(BF16))
    return jnp.concatenate(parts, axis=1)


def store_position(spread, position, positions, rows):
    for h in range(spread.shape[0]):
        part = rows[:, h * LANES : (h + 1) * LANES]
        spread[h, pl.ds(position, rows.shape[0], stride=positions), :] = part


def widen(source, spread):
    for h in range(spread.shape[0]):
        part = source[:, :, h * LANES : (h + 1) * LANES].astype(F32)
        spread[h] = part.reshape(spread.shape[1], LANES)


def send_kernel(field, out, held, sems):
    frames = field.shape[0]
    arrive = [
        pltpu.make_async_copy(field.at[f], held.at[f], sems.at[0, f]) for f in range(frames)
    ]
    leave = [
        pltpu.make_async_copy(held.at[f], out.at[:, f], sems.at[1, f]) for f in range(frames)
    ]
    for copy in arrive:
        copy.start()
    for f in range(frames):
        arrive[f].wait()
        leave[f].start()
    for copy in leave:
        copy.wait()


def grads_kernel(
    cotangent, used, w_out, w_query, w_key, w_value, folded, mixed, spread, ordered, attended
):
    all_frames, positions, channels = cotangent.shape
    mixed[...] = (dot(w_query[...], w_key[...], (1, 1)) * channels ** (-0.5)).astype(BF16)
    widen(cotangent, spread)
    for first in range(0, positions, GROUP):
        for p in range(first, first + GROUP):
            here = slice(p * all_frames, (p + 1) * all_frames)
            ordered[here] = load_position(spread, p, positions, used[...])
        here = slice(first * all_frames, (first + GROUP) * all_frames)
        attended[here] = dot(ordered[here], w_out[...], (1, 1)).astype(BF16)
        grads = dot(attended[here], w_value[...], (1, 1)).astype(BF16)
        folded[first : first + GROUP] = grads.reshape(GROUP, all_frames, channels)


def softmax_probs(query, key, allowed, scale):
    scores = jnp.where(allowed, dot(key, query, (1, 1)) * scale, -1e30)
    expo = jnp.exp(scores - jnp.max(scores, axis=0, keepdims=True))
    return expo * (1.0 / jnp.sum(expo, axis=0, keepdims=True))


def allowed_pairs(used):
    tile = (used.shape[0], used.shape[0])
    source = lax.broadcasted_iota(jnp.int32, tile, 0)
    reader = lax.broadcasted_iota(jnp.int32, tile, 1)
    return (source <= reader) & (used[...] > 0.0)


def attention_kernel(
    normed, folded, used, mixed, grad_normed, kept,
    weights, bias, result, out, ordered, sides, products, mix, inner, direct, sems,
):
    all_frames, positions, channels = normed.shape
    pieces = positions // GROUP
    loads = [
        pltpu.make_async_copy(mixed, weights, sems.at[0]),
        pltpu.make_async_copy(folded, sides.at[:, all_frames:], sems.at[1]),
    ]
    for copy in loads:
        copy.start()
    for f in range(0, all_frames, TILE):
        ordered[:, f : f + TILE] = jnp.transpose(normed[f : f + TILE], (1, 0, 2))
    bias[...] = jnp.where(allowed_pairs(used), 0.0, -1e30)
    keep = pltpu.make_async_copy(ordered, kept, sems.at[2 * pieces - 1])
    keep.start()

    def rows_of(p):
        return slice(p * all_frames, (p + 1) * all_frames)

    def group_of(first):
        return slice(first * all_frames, (first + GROUP) * all_frames)

    def project_group(first):
        rows = ordered[first : first + GROUP].reshape(GROUP * all_frames, channels)
        queries = dot(rows, weights[...]).astype(BF16)
        sides[first : first + GROUP, :all_frames] = queries.reshape(GROUP, all_frames, channels)

    def pair_products(p):
        products[p] = dot(ordered[p], sides[p], (1, 1))

    def softmax(p):
        logits = products[p, :, :all_frames] + bias[...]
        expo = jnp.exp(logits - jnp.max(logits, axis=0, keepdims=True))
        probs = expo * (1.0 / jnp.sum(expo, axis=0, keepdims=True))
        low = probs.astype(BF16)
        grad = products[p, :, all_frames:]
        delta = jnp.sum(low.astype(F32) * grad, axis=0, keepdims=True)
        mix[p, :, :all_frames] = (probs * (grad - delta)).astype(BF16)
        mix[p, :, all_frames:] = low

    def back_products(p):
        here = rows_of(p)
        direct[here] = dot(mix[p], sides[p])
        inner[here] = dot(mix[p, :, :all_frames], ordered[p], (0, 0)).astype(BF16)

    def back_group(first):
        group = group_of(first)
        total = dot(inner[group], weights[...], (1, 1)) + direct[group]
        result[first : first + GROUP] = total.astype(BF16).reshape(GROUP, all_frames, channels)

    loads[0].wait()
    project_group(0)
    loads[1].wait()
    for first in range(0, positions, GROUP):
        group = range(first, first + GROUP)
        for p in group:
            pair_products(p)
            if first > 0:
                back_products(p - GROUP)
        if first + GROUP < positions:
            project_group(first + GROUP)
        if first > 0:
            back_group(first - GROUP)
        for p in group:
            softmax(p)
    for p in range(positions - GROUP, positions):
        back_products(p)
    back_group(positions - GROUP)
    copies = []
    size = all_frames // pieces
    for i in range(pieces):
        for f in range(i * size, (i + 1) * size, TILE):
            out[f : f + TILE] = jnp.transpose(result[:, f : f + TILE], (1, 0, 2))
        here = slice(i * size, (i + 1) * size)
        copy = pltpu.make_async_copy(out.at[here], grad_normed.at[here], sems.at[i])
        copy.start()
        copies.append(copy)
    for copy in copies + [keep]:
        copy.wait()


def project_kernel(
    ordered, used, w_query, w_key, w_value, w_out, projected,
    spread, query_s, key_s, value_s, attended,
):
    all_frames, positions, channels = projected.shape
    allowed = allowed_pairs(used)
    scale = channels ** (-0.5)

    def step(i, carry):
        first = pl.multiple_of(i * GROUP * all_frames, GROUP * all_frames)
        rows = ordered[pl.ds(first, GROUP * all_frames)]
        query_s[...] = dot(rows, w_query[...]).astype(BF16)
        key_s[...] = dot(rows, w_key[...]).astype(BF16)
        value_s[...] = dot(rows, w_value[...]).astype(BF16)
        for j in range(GROUP):
            here = slice(j * all_frames, (j + 1) * all_frames)
            low = softmax_probs(query_s[here], key_s[here], allowed, scale).astype(BF16)
            attended[here] = dot(low, value_s[here], (0, 0)).astype(BF16)
        total = dot(attended[...], w_out[...]).astype(BF16).astype(F32)
        for j in range(GROUP):
            part = total[j * all_frames : (j + 1) * all_frames]
            store_position(spread, i * GROUP + j, positions, part)
        return carry

    lax.fori_loop(0, positions // GROUP, step, 0)
    for h in range(spread.shape[0]):
        part = spread[h].reshape(all_frames, positions, LANES)
        projected[:, :, h * LANES : (h + 1) * LANES] = part.astype(BF16)


def encode_kernel(frame_count, row_count, hidden, projected, encoded, held, sems):
    frames_here = frame_count[lax.axis_index("tm")]
    rows_here = row_count[lax.axis_index("space")]
    frames, slots, columns, channels = encoded.shape
    tokens = slots * columns
    copies = []
    for frame in range(frames):
        total = hidden[:, frame].astype(F32) + projected[:, frame].astype(F32)
        total = total.reshape(tokens, channels)
        used = token_mask(frame, frames_here, rows_here, columns, total.shape)
        total = jnp.where(used, total, 0.0).astype(BF16)
        held[frame] = total.reshape(slots, columns, channels)
        copy = pltpu.make_async_copy(held.at[frame], encoded.at[frame], sems.at[frame])
        copy.start()
        copies.append(copy)
    for copy in copies:
        copy.wait()


def grad_hidden_kernel(
    frame_count, row_count, cotangent, hidden, grad_normed, grad_hidden, head, tail
):
    frames_here = frame_count[lax.axis_index("tm")]
    rows_here = row_count[lax.axis_index("space")]
    frames, slots, columns, channels = cotangent.shape
    tokens = slots * columns

    def step(frame, carry):
        hid = hidden[:, frame].astype(F32).reshape(tokens, channels)
        grad = grad_normed[:, frame].astype(F32).reshape(tokens, channels)
        outer = cotangent[frame].astype(F32).reshape(tokens, channels)
        inv = inverse_rms(hid)
        inner = jnp.mean(grad * hid, axis=-1, keepdims=True)
        total = outer + inv * grad - (inv * inv * inv * inner) * hid
        used = token_mask(frame, frames_here, rows_here, columns, total.shape)
        total = jnp.where(used, total, 0.0).astype(BF16)
        grad_hidden[frame] = total.reshape(slots, columns, channels)
        return carry

    lax.fori_loop(0, frames, step, 0)
    head[...] = grad_hidden[:, 0]
    tail[...] = grad_hidden[:, rows_here - 1]


def video_grad_kernel(frame_count, row_count, field, above, below, weight, out, extended):
    frames_here = frame_count[lax.axis_index("tm")]
    rows_here = row_count[lax.axis_index("space")]
    frames, slots, columns, channels = field.shape
    tokens = slots * columns
    fill_halo(extended, field, above, below, rows_here)

    def step(frame, carry):
        total = convolve_frame(extended, weight, frame, True)
        used = token_mask(frame, frames_here, rows_here, columns, total.shape)
        center = field[frame].reshape(tokens, channels).astype(F32)
        total = jnp.where(used, center + total, 0.0).astype(BF16)
        out[frame] = total.reshape(slots, columns, channels)
        return carry

    lax.fori_loop(0, frames, step, 0)


def share_rows(head, tail):
    ends = lax.axis_size("space") - 1
    above = lax.ppermute(tail, "space", [(i, i + 1) for i in range(ends)])
    below = lax.ppermute(head, "space", [(i + 1, i) for i in range(ends)])
    return above, below


def exchange(blocks):
    return lax.all_to_all(blocks, "tm", split_axis=0, concat_axis=0, tiled=True)


def body(video, cotangent, frame_count, row_count, w_conv, w_query, w_key, w_value, w_out):
    frames, slots, columns, channels = video.shape
    blocks = lax.axis_size("tm")
    positions = slots * columns // blocks
    all_frames = frames * blocks
    shaped = jax.ShapeDtypeStruct
    home = (frames, slots, columns, channels)
    sent = (blocks, frames, positions, channels)
    spread = (all_frames, positions, channels)
    ordered = (positions, all_frames, channels)
    edge = (frames, columns, channels)
    padded = (frames, slots + 2, columns, channels)
    size = 2 * frames * slots * columns * channels
    product = 2 * frames * slots * columns * channels * channels
    inner = 2 * positions * all_frames * all_frames * channels

    def call(kernel, outs, ins, args, scratch, flops, moved, out_spaces=None):
        args = [
            pltpu.with_memory_space_constraint(x, VMEM) if space is ON_CHIP else x
            for x, space in zip(args, ins)
        ]
        ins = [VMEM if space is ON_CHIP else space for space in ins]
        return pl.pallas_call(
            kernel,
            out_shape=outs,
            in_specs=specs(*ins),
            out_specs=specs(*(out_spaces or [VMEM] * len(outs))),
            scratch_shapes=scratch,
            cost_estimate=cost(flops, moved),
        )(*args)

    dma = pltpu.SemaphoreType.DMA
    wide = VMEM((channels // LANES, all_frames * positions, LANES), F32)
    flat = VMEM((all_frames * positions, channels), BF16)
    part = VMEM((GROUP * all_frames, channels), BF16)
    chunked = (frames, blocks, positions, channels)

    (outgoing,) = call(
        send_kernel, [shaped(sent, BF16)], [HBM], [cotangent.reshape(chunked)],
        [VMEM(chunked, BF16), dma((2, frames))], 0, size, [HBM],
    )
    grads_in = exchange(outgoing).reshape(spread)
    head, tail = call(
        edges_kernel, [VMEM(edge, BF16)] * 2, [SMEM, HBM], [row_count, video],
        [dma((2,))], 0, size // 4,
    )
    above, below = share_rows(head, tail)
    hidden, normed = call(
        hidden_kernel, [shaped(sent, BF16)] * 2, [SMEM, SMEM, VMEM, ON_CHIP, ON_CHIP, VMEM],
        [frame_count, row_count, video, above, below, w_conv], [VMEM(padded, BF16)],
        9 * product, 4 * size,
    )
    normed_in = exchange(normed).reshape(spread)
    slot = lax.broadcasted_iota(jnp.int32, (blocks, frames, LANES), 1)
    used = (slot < frame_count[:, None, None]).astype(F32).reshape(all_frames, LANES)
    folded, mixed = call(
        grads_kernel, [shaped(ordered, BF16), shaped((channels, channels), BF16)],
        [ON_CHIP, ON_CHIP] + [VMEM] * 4, [grads_in, used, w_out, w_query, w_key, w_value],
        [wide, flat, flat], 2 * product, 2 * size,
    )
    pairs = (all_frames, all_frames)
    double = (positions, 2 * all_frames, channels)
    grad_normed, kept = call(
        attention_kernel,
        [shaped(spread, BF16), shaped(ordered, BF16)],
        [ON_CHIP, HBM, ON_CHIP, HBM], [normed_in, folded, used, mixed],
        [
            VMEM((channels, channels), BF16), VMEM(pairs, F32), VMEM(ordered, BF16), VMEM(spread, BF16),
            VMEM(ordered, BF16), VMEM(double, BF16), VMEM((positions, all_frames, 2 * all_frames), F32),
            VMEM((positions, all_frames, 2 * all_frames), BF16), flat,
            VMEM((all_frames * positions, channels), F32), dma((2 * positions // GROUP,)),
        ],
        2 * product + 5 * inner, 4 * size, [HBM, HBM],
    )
    grad_home = exchange(grad_normed.reshape(sent))
    (projected,) = call(
        project_kernel, [shaped(spread, BF16)], [VMEM, ON_CHIP] + [VMEM] * 4,
        [kept.reshape(all_frames * positions, channels), used, w_query, w_key, w_value, w_out],
        [wide] + [part] * 4, 4 * product + 2 * inner, 2 * size,
    )
    projected_home = exchange(projected.reshape(sent))
    grad_hidden, head, tail = call(
        grad_hidden_kernel, [shaped(home, BF16), shaped(edge, BF16), shaped(edge, BF16)],
        [SMEM, SMEM, VMEM, VMEM, ON_CHIP],
        [frame_count, row_count, cotangent, hidden, grad_home], [], 0, 5 * size,
    )
    above, below = share_rows(head, tail)
    (video_grad,) = call(
        video_grad_kernel, [shaped(home, BF16)], [SMEM, SMEM, VMEM, ON_CHIP, ON_CHIP, VMEM],
        [frame_count, row_count, grad_hidden, above, below, w_conv], [VMEM(padded, BF16)],
        9 * product, 3 * size,
    )
    (encoded,) = call(
        encode_kernel, [shaped(home, BF16)], [SMEM, SMEM, ON_CHIP, ON_CHIP],
        [frame_count, row_count, hidden, projected_home],
        [VMEM(home, BF16), dma((frames,))], 0, 3 * size, [HBM],
    )
    return encoded, video_grad


def solution(mesh):
    field = P("tm", "space", None, None)
    in_specs = (field, field) + (P(),) * 7

    return jax.shard_map(
        body, mesh=mesh, in_specs=in_specs, out_specs=(field, field), check_vma=False
    )
```

```python
import jax
import jax.numpy as jnp
from jax import lax
from jax.experimental import pallas as pl
from jax.experimental.pallas import tpu as pltpu
from jax.sharding import PartitionSpec as P


BF16 = jnp.bfloat16
F32 = jnp.float32
GROUP = 4
LANES = 128
TILE = 16
PIECES = 4
VMEM = pltpu.VMEM
SMEM = pltpu.SMEM
HBM = pltpu.HBM
ON_CHIP = object()


def dot(a, b, contract=(1, 0)):
    return lax.dot_general(
        a, b, (((contract[0],), (contract[1],)), ((), ())), preferred_element_type=F32
    )


def specs(*spaces):
    return [pl.BlockSpec(memory_space=space) for space in spaces]


def cost(flops, moved):
    return pl.CostEstimate(flops=flops, bytes_accessed=moved, transcendentals=0)


def edges_kernel(row_count, field, head, tail, sems):
    rows_here = row_count[lax.axis_index("space")]
    first = pltpu.make_async_copy(field.at[:, 0], head, sems.at[0])
    last = pltpu.make_async_copy(field.at[:, rows_here - 1], tail, sems.at[1])
    first.start()
    last.start()
    first.wait()
    last.wait()


def fill_halo(extended, field, above, below, rows_here):
    slots = field.shape[1]
    extended[:, 1 : 1 + slots] = field[...]
    extended[:, 0] = above[...]
    extended[:, 1 + rows_here] = below[...]


def convolve_frame(extended, weight, frame, flipped):
    _, padded, columns, channels = extended.shape
    tokens = (padded - 2) * columns
    column = lax.broadcasted_iota(jnp.int32, (tokens, channels), 0) % columns
    total = None
    for b in range(3):
        part = None
        for a in range(3):
            view = extended[frame, a : a + padded - 2].reshape(tokens, channels)
            if flipped:
                term = dot(view, weight[2 - a, 2 - b], (1, 1))
            else:
                term = dot(view, weight[a, b])
            part = term if part is None else part + term
        if b == 0:
            part = jnp.where(column == 0, 0.0, pltpu.roll(part, 1, 0))
        elif b == 2:
            part = jnp.where(column == columns - 1, 0.0, pltpu.roll(part, tokens - 1, 0))
        total = part if total is None else total + part
    return total


def token_mask(frame, frames_here, rows_here, columns, shape):
    row = lax.broadcasted_iota(jnp.int32, shape, 0) // columns
    return (row < rows_here) & (frame < frames_here)


def inverse_rms(hidden):
    return lax.rsqrt(jnp.mean(hidden * hidden, axis=-1, keepdims=True) + 1e-06)


def hidden_kernel(
    frame_count, row_count, field, above, below, weight, hidden_out, normed_out, extended
):
    frames_here = frame_count[lax.axis_index("tm")]
    rows_here = row_count[lax.axis_index("space")]
    frames, slots, columns, channels = field.shape
    tokens = slots * columns
    fill_halo(extended, field, above, below, rows_here)

    def step(frame, carry):
        total = convolve_frame(extended, weight, frame, False)
        used = token_mask(frame, frames_here, rows_here, columns, total.shape)
        center = field[frame].reshape(tokens, channels).astype(F32)
        hidden = jnp.where(used, center + total, 0.0).astype(BF16)
        hidden_out[:, frame] = hidden.reshape(hidden_out.shape[0], -1, channels)
        hidden_f = hidden.astype(F32)
        normed = (hidden_f * inverse_rms(hidden_f)).astype(BF16)
        normed_out[:, frame] = normed.reshape(normed_out.shape[0], -1, channels)
        return carry

    lax.fori_loop(0, frames, step, 0)


def load_position(spread, position, positions, scale=None):
    parts = []
    for h in range(spread.shape[0]):
        rows = spread[h, pl.ds(position, spread.shape[1] // positions, stride=positions), :]
        parts.append((rows if scale is None else rows * scale).astype(BF16))
    return jnp.concatenate(parts, axis=1)


def store_position(spread, position, positions, rows):
    for h in range(spread.shape[0]):
        part = rows[:, h * LANES : (h + 1) * LANES]
        spread[h, pl.ds(position, rows.shape[0], stride=positions), :] = part


def widen(source, spread):
    for h in range(spread.shape[0]):
        part = source[:, :, h * LANES : (h + 1) * LANES].astype(F32)
        spread[h] = part.reshape(spread.shape[1], LANES)


def send_kernel(field, out, held, sems):
    frames, blocks = field.shape[:2]
    size = blocks // PIECES
    pieces = [(f, pl.ds(i * size, size), i) for f in range(frames) for i in range(PIECES)]
    arrive = [
        pltpu.make_async_copy(field.at[f, at], held.at[f, at], sems.at[0, f, i])
        for f, at, i in pieces
    ]
    leave = [
        pltpu.make_async_copy(held.at[f, at], out.at[at, f], sems.at[1, f, i])
        for f, at, i in pieces
    ]
    for copy in arrive:
        copy.start()
    for first, second in zip(arrive, leave):
        first.wait()
        second.start()
    for copy in leave:
        copy.wait()


def grads_kernel(
    cotangent, used, w_out, w_query, w_key, w_value, folded, mixed, spread, ordered, attended
):
    all_frames, positions, channels = cotangent.shape
    mixed[...] = (dot(w_query[...], w_key[...], (1, 1)) * channels ** (-0.5)).astype(BF16)
    widen(cotangent, spread)
    for first in range(0, positions, GROUP):
        for p in range(first, first + GROUP):
            here = slice(p * all_frames, (p + 1) * all_frames)
            ordered[here] = load_position(spread, p, positions, used[...])
        here = slice(first * all_frames, (first + GROUP) * all_frames)
        attended[here] = dot(ordered[here], w_out[...], (1, 1)).astype(BF16)
        grads = dot(attended[here], w_value[...], (1, 1)).astype(BF16)
        folded[first : first + GROUP] = grads.reshape(GROUP, all_frames, channels)


def softmax_probs(query, key, allowed, scale):
    scores = jnp.where(allowed, dot(key, query, (1, 1)) * scale, -1e30)
    expo = jnp.exp(scores - jnp.max(scores, axis=0, keepdims=True))
    return expo * (1.0 / jnp.sum(expo, axis=0, keepdims=True))


def allowed_pairs(used):
    tile = (used.shape[0], used.shape[0])
    source = lax.broadcasted_iota(jnp.int32, tile, 0)
    reader = lax.broadcasted_iota(jnp.int32, tile, 1)
    return (source <= reader) & (used[...] > 0.0)


def attention_kernel(
    normed, folded, used, mixed, grad_normed, kept,
    weights, bias, result, out, ordered, sides, products, mix, inner, direct, sems,
):
    all_frames, positions, channels = normed.shape
    pieces = positions // GROUP
    loads = [
        pltpu.make_async_copy(mixed, weights, sems.at[0]),
        pltpu.make_async_copy(folded, sides.at[:, all_frames:], sems.at[1]),
    ]
    for copy in loads:
        copy.start()
    for f in range(0, all_frames, TILE):
        ordered[:, f : f + TILE] = jnp.transpose(normed[f : f + TILE], (1, 0, 2))
    bias[...] = jnp.where(allowed_pairs(used), 0.0, -1e30)
    keep = pltpu.make_async_copy(ordered, kept, sems.at[2 * pieces - 1])
    keep.start()

    def rows_of(p):
        return slice(p * all_frames, (p + 1) * all_frames)

    def group_of(first):
        return slice(first * all_frames, (first + GROUP) * all_frames)

    def project_group(first):
        rows = ordered[first : first + GROUP].reshape(GROUP * all_frames, channels)
        queries = dot(rows, weights[...]).astype(BF16)
        sides[first : first + GROUP, :all_frames] = queries.reshape(GROUP, all_frames, channels)

    def pair_products(p):
        products[p] = dot(ordered[p], sides[p], (1, 1))

    def softmax(p):
        logits = products[p, :, :all_frames] + bias[...]
        expo = jnp.exp(logits - jnp.max(logits, axis=0, keepdims=True))
        probs = expo * (1.0 / jnp.sum(expo, axis=0, keepdims=True))
        low = probs.astype(BF16)
        grad = products[p, :, all_frames:]
        delta = jnp.sum(low.astype(F32) * grad, axis=0, keepdims=True)
        mix[p, :, :all_frames] = (probs * (grad - delta)).astype(BF16)
        mix[p, :, all_frames:] = low

    def back_products(p):
        here = rows_of(p)
        direct[here] = dot(mix[p], sides[p])
        inner[here] = dot(mix[p, :, :all_frames], ordered[p], (0, 0)).astype(BF16)

    def back_group(first):
        group = group_of(first)
        total = dot(inner[group], weights[...], (1, 1)) + direct[group]
        result[first : first + GROUP] = total.astype(BF16).reshape(GROUP, all_frames, channels)

    loads[0].wait()
    project_group(0)
    loads[1].wait()
    for first in range(0, positions, GROUP):
        group = range(first, first + GROUP)
        for p in group:
            pair_products(p)
            if first > 0:
                back_products(p - GROUP)
        if first + GROUP < positions:
            project_group(first + GROUP)
        if first > 0:
            back_group(first - GROUP)
        for p in group:
            softmax(p)
    for p in range(positions - GROUP, positions):
        back_products(p)
    back_group(positions - GROUP)
    copies = []
    size = all_frames // pieces
    for i in range(pieces):
        for f in range(i * size, (i + 1) * size, TILE):
            out[f : f + TILE] = jnp.transpose(result[:, f : f + TILE], (1, 0, 2))
        here = slice(i * size, (i + 1) * size)
        copy = pltpu.make_async_copy(out.at[here], grad_normed.at[here], sems.at[i])
        copy.start()
        copies.append(copy)
    for copy in copies + [keep]:
        copy.wait()


def project_kernel(
    ordered, used, w_query, w_key, w_value, w_out, projected,
    spread, query_s, key_s, value_s, attended,
):
    all_frames, positions, channels = projected.shape
    allowed = allowed_pairs(used)
    scale = channels ** (-0.5)

    def step(i, carry):
        first = pl.multiple_of(i * GROUP * all_frames, GROUP * all_frames)
        rows = ordered[pl.ds(first, GROUP * all_frames)]
        query_s[...] = dot(rows, w_query[...]).astype(BF16)
        key_s[...] = dot(rows, w_key[...]).astype(BF16)
        value_s[...] = dot(rows, w_value[...]).astype(BF16)
        for j in range(GROUP):
            here = slice(j * all_frames, (j + 1) * all_frames)
            low = softmax_probs(query_s[here], key_s[here], allowed, scale).astype(BF16)
            attended[here] = dot(low, value_s[here], (0, 0)).astype(BF16)
        total = dot(attended[...], w_out[...]).astype(BF16).astype(F32)
        for j in range(GROUP):
            part = total[j * all_frames : (j + 1) * all_frames]
            store_position(spread, i * GROUP + j, positions, part)
        return carry

    lax.fori_loop(0, positions // GROUP, step, 0)
    for h in range(spread.shape[0]):
        part = spread[h].reshape(all_frames, positions, LANES)
        projected[:, :, h * LANES : (h + 1) * LANES] = part.astype(BF16)


def encode_kernel(frame_count, row_count, hidden, projected, encoded, held, sems):
    frames_here = frame_count[lax.axis_index("tm")]
    rows_here = row_count[lax.axis_index("space")]
    frames, slots, columns, channels = encoded.shape
    half = slots // 2
    groups = hidden.shape[0] // 2
    tokens = half * columns
    copies = []
    for frame in range(frames):
        for i in range(2):
            source = slice(i * groups, (i + 1) * groups)
            rows = slice(i * half, (i + 1) * half)
            total = hidden[source, frame].astype(F32) + projected[source, frame].astype(F32)
            total = total.reshape(tokens, channels)
            used = token_mask(frame, frames_here, rows_here - i * half, columns, total.shape)
            total = jnp.where(used, total, 0.0).astype(BF16)
            held[frame, rows] = total.reshape(half, columns, channels)
            copy = pltpu.make_async_copy(
                held.at[frame, rows], encoded.at[frame, rows], sems.at[frame, i]
            )
            copy.start()
            copies.append(copy)
    for copy in copies:
        copy.wait()


def grad_hidden_kernel(
    frame_count, row_count, cotangent, hidden, grad_normed, grad_hidden, head, tail
):
    frames_here = frame_count[lax.axis_index("tm")]
    rows_here = row_count[lax.axis_index("space")]
    frames, slots, columns, channels = cotangent.shape
    tokens = slots * columns

    def step(frame, carry):
        hid = hidden[:, frame].astype(F32).reshape(tokens, channels)
        grad = grad_normed[:, frame].astype(F32).reshape(tokens, channels)
        outer = cotangent[frame].astype(F32).reshape(tokens, channels)
        inv = inverse_rms(hid)
        inner = jnp.mean(grad * hid, axis=-1, keepdims=True)
        total = outer + inv * grad - (inv * inv * inv * inner) * hid
        used = token_mask(frame, frames_here, rows_here, columns, total.shape)
        total = jnp.where(used, total, 0.0).astype(BF16)
        grad_hidden[frame] = total.reshape(slots, columns, channels)
        return carry

    lax.fori_loop(0, frames, step, 0)
    head[...] = grad_hidden[:, 0]
    tail[...] = grad_hidden[:, rows_here - 1]


def video_grad_kernel(frame_count, row_count, field, above, below, weight, out, extended):
    frames_here = frame_count[lax.axis_index("tm")]
    rows_here = row_count[lax.axis_index("space")]
    frames, slots, columns, channels = field.shape
    tokens = slots * columns
    fill_halo(extended, field, above, below, rows_here)

    def step(frame, carry):
        total = convolve_frame(extended, weight, frame, True)
        used = token_mask(frame, frames_here, rows_here, columns, total.shape)
        center = field[frame].reshape(tokens, channels).astype(F32)
        total = jnp.where(used, center + total, 0.0).astype(BF16)
        out[frame] = total.reshape(slots, columns, channels)
        return carry

    lax.fori_loop(0, frames, step, 0)


def share_rows(head, tail):
    ends = lax.axis_size("space") - 1
    above = lax.ppermute(tail, "space", [(i, i + 1) for i in range(ends)])
    below = lax.ppermute(head, "space", [(i + 1, i) for i in range(ends)])
    return above, below


def exchange(blocks):
    return lax.all_to_all(blocks, "tm", split_axis=0, concat_axis=0, tiled=True)


def body(video, cotangent, frame_count, row_count, w_conv, w_query, w_key, w_value, w_out):
    frames, slots, columns, channels = video.shape
    blocks = lax.axis_size("tm")
    positions = slots * columns // blocks
    all_frames = frames * blocks
    shaped = jax.ShapeDtypeStruct
    home = (frames, slots, columns, channels)
    sent = (blocks, frames, positions, channels)
    spread = (all_frames, positions, channels)
    ordered = (positions, all_frames, channels)
    edge = (frames, columns, channels)
    padded = (frames, slots + 2, columns, channels)
    size = 2 * frames * slots * columns * channels
    product = 2 * frames * slots * columns * channels * channels
    inner = 2 * positions * all_frames * all_frames * channels

    def call(kernel, outs, ins, args, scratch, flops, moved, out_spaces=None):
        args = [
            pltpu.with_memory_space_constraint(x, VMEM) if space is ON_CHIP else x
            for x, space in zip(args, ins)
        ]
        ins = [VMEM if space is ON_CHIP else space for space in ins]
        return pl.pallas_call(
            kernel,
            out_shape=outs,
            in_specs=specs(*ins),
            out_specs=specs(*(out_spaces or [VMEM] * len(outs))),
            scratch_shapes=scratch,
            cost_estimate=cost(flops, moved),
        )(*args)

    dma = pltpu.SemaphoreType.DMA
    wide = VMEM((channels // LANES, all_frames * positions, LANES), F32)
    flat = VMEM((all_frames * positions, channels), BF16)
    part = VMEM((GROUP * all_frames, channels), BF16)
    chunked = (frames, blocks, positions, channels)

    (outgoing,) = call(
        send_kernel, [shaped(sent, BF16)], [HBM], [cotangent.reshape(chunked)],
        [VMEM(chunked, BF16), dma((2, frames, PIECES))], 0, size, [HBM],
    )
    grads_in = exchange(outgoing).reshape(spread)
    head, tail = call(
        edges_kernel, [VMEM(edge, BF16)] * 2, [SMEM, HBM], [row_count, video],
        [dma((2,))], 0, size // 4,
    )
    above, below = share_rows(head, tail)
    hidden, normed = call(
        hidden_kernel, [shaped(sent, BF16)] * 2, [SMEM, SMEM, VMEM, ON_CHIP, ON_CHIP, VMEM],
        [frame_count, row_count, video, above, below, w_conv], [VMEM(padded, BF16)],
        9 * product, 4 * size,
    )
    normed_in = exchange(normed).reshape(spread)
    slot = lax.broadcasted_iota(jnp.int32, (blocks, frames, LANES), 1)
    used = (slot < frame_count[:, None, None]).astype(F32).reshape(all_frames, LANES)
    folded, mixed = call(
        grads_kernel, [shaped(ordered, BF16), shaped((channels, channels), BF16)],
        [ON_CHIP, ON_CHIP] + [VMEM] * 4, [grads_in, used, w_out, w_query, w_key, w_value],
        [wide, flat, flat], 2 * product, 2 * size,
    )
    pairs = (all_frames, all_frames)
    double = (positions, 2 * all_frames, channels)
    grad_normed, kept = call(
        attention_kernel,
        [shaped(spread, BF16), shaped(ordered, BF16)],
        [ON_CHIP, HBM, ON_CHIP, HBM], [normed_in, folded, used, mixed],
        [
            VMEM((channels, channels), BF16), VMEM(pairs, F32), VMEM(ordered, BF16), VMEM(spread, BF16),
            VMEM(ordered, BF16), VMEM(double, BF16), VMEM((positions, all_frames, 2 * all_frames), F32),
            VMEM((positions, all_frames, 2 * all_frames), BF16), flat,
            VMEM((all_frames * positions, channels), F32), dma((2 * positions // GROUP,)),
        ],
        2 * product + 5 * inner, 4 * size, [HBM, HBM],
    )
    grad_home = exchange(grad_normed.reshape(sent))
    (projected,) = call(
        project_kernel, [shaped(spread, BF16)], [VMEM, ON_CHIP] + [VMEM] * 4,
        [kept.reshape(all_frames * positions, channels), used, w_query, w_key, w_value, w_out],
        [wide] + [part] * 4, 4 * product + 2 * inner, 2 * size,
    )
    projected_home = exchange(projected.reshape(sent))
    grad_hidden, head, tail = call(
        grad_hidden_kernel, [shaped(home, BF16), shaped(edge, BF16), shaped(edge, BF16)],
        [SMEM, SMEM, VMEM, VMEM, ON_CHIP],
        [frame_count, row_count, cotangent, hidden, grad_home], [], 0, 5 * size,
    )
    above, below = share_rows(head, tail)
    (video_grad,) = call(
        video_grad_kernel, [shaped(home, BF16)], [SMEM, SMEM, VMEM, ON_CHIP, ON_CHIP, VMEM],
        [frame_count, row_count, grad_hidden, above, below, w_conv], [VMEM(padded, BF16)],
        9 * product, 3 * size,
    )
    (encoded,) = call(
        encode_kernel, [shaped(home, BF16)], [SMEM, SMEM, ON_CHIP, ON_CHIP],
        [frame_count, row_count, hidden, projected_home],
        [VMEM(home, BF16), dma((frames, 2))], 0, 3 * size, [HBM],
    )
    return encoded, video_grad


def solution(mesh):
    field = P("tm", "space", None, None)
    in_specs = (field, field) + (P(),) * 7

    return jax.shard_map(
        body, mesh=mesh, in_specs=in_specs, out_specs=(field, field), check_vma=False
    )
```
